32 devices in a mesh: depth: 8 (over z, y), lat: 4 (over x, core).
Axes of the slice: x: 2, y: 2, z: 4, core: 2. Of those that a mesh axis runs over, the one named last changes fastest.
Arguments:
- right_sides: bfloat16 [16, 2, 64, 3072], P('depth', None, None, 'lat'), may hold values from -6 to 6
- sources: int32 [64], replicated, may hold values from 0 to 3071
- coupling: float32 [16, 3072], P('depth', 'lat'), may hold values from 0.76 to 0.86
- block_cols: int32 [16, 24, 4], P('depth', 'lat'), may hold values from 0 to 23, as said below
- factors: bfloat16 [16, 24, 4, 2, 128, 128], P('depth', 'lat'), may hold values from -0.2 to 1.2
Outputs:
- solution: bfloat16 [16, 2, 64, 3072], P('depth', None, None, 'lat')
The draws below stay inside these ranges and needn't reach their ends.
Inputs may be any that keep to these rules, and one draw needn't show every extreme that they name: block_cols[k, r, 0] is r; the entries of a row are distinct and within 3 of r.
All inputs are finite; a program needn't handle non-finite values.
Results may differ from the reference program's by a relative error of at most 0.03.
Values may be sent and summed in bfloat16 or wider, within the bound.
A program may use at most 64 MiB of HBM per device.

```python
import math
import jax
import jax.numpy as jnp
from jax import lax

BLOCK = 128
NNZ = 4
REACH = 3
SHOTS = 64
NBLK = 24
PLANE = 3072
LAYERS = 16


def draw_coupling(key, part):
    shape = (LAYERS, PLANE)
    unit = jax.random.uniform(key, shape, jnp.float32, 0.0, 1.0)
    values = 0.76 + 0.1 * unit
    return jnp.clip(values, 0.76, 0.86).astype(jnp.float32)


def draw_block_cols(key, part):
    width = 2 * REACH + 1
    offsets = jnp.arange(width, dtype=jnp.int32) - REACH
    row_ids = jnp.arange(NBLK, dtype=jnp.int32)
    candidate = jnp.broadcast_to(row_ids[None, :, None] + offsets[None, None, :], (LAYERS, NBLK, width))
    noise = jax.random.randint(key, (LAYERS, NBLK, width), 0, 1000)
    score = noise * width + jnp.arange(width, dtype=jnp.int32)[None, None, :]
    inside = (candidate >= 0) & (candidate < NBLK)
    score = jnp.where(offsets[None, None, :] == 0, 10000000, jnp.where(inside, score, -1))
    _, chosen = lax.top_k(score, NNZ)
    return jnp.take_along_axis(candidate, chosen, axis=-1).astype(jnp.int32)


def draw_factors(key, part):
    shape = (LAYERS, NBLK, NNZ, 2, BLOCK, BLOCK)
    sigma = 0.5 / math.sqrt(2.0 * NNZ * BLOCK)
    noise = jax.random.normal(key, shape, jnp.float32) * sigma
    noise = jnp.clip(noise, -6.0 * sigma, 6.0 * sigma)
    identity = jnp.eye(BLOCK, dtype=jnp.float32)
    leading = ((jnp.arange(NNZ) == 0)[:, None] & (jnp.arange(2) == 0)[None, :]).astype(jnp.float32)
    return (noise + leading[None, None, :, :, None, None] * identity).astype(jnp.bfloat16)


def plant(entries, key, low, largest):
    longest = entries.shape.index(max(entries.shape))
    spots = []
    for shift in (0, 1):
        where = [jax.random.randint(jax.random.fold_in(key, axis), (), 0, length) for axis, length in enumerate(entries.shape)]
        where[longest] = (where[longest] + shift) % entries.shape[longest]
        spots.append(tuple(where))
    return entries.at[spots[0]].set(low).at[spots[1]].set(largest)


def block_scale(key, dims, cuts, low, largest):
    def one(position, shards_of):
        steps = jax.random.uniform(jax.random.fold_in(jax.random.fold_in(key, 6), position), (shards_of,), jnp.float32, low / len(cuts), largest / len(cuts))
        return jnp.repeat(jnp.exp(steps), dims[position] // shards_of).reshape((-1,) + (1,) * (len(dims) - position - 1))

    loudness = one(*cuts[0])
    for cut in cuts[1:]:
        loudness = loudness * one(*cut)
    return loudness


def gaussian(rng, shape, scale, reach, cuts=(), held_as=jnp.bfloat16):
    factor_of = block_scale(rng, shape, cuts, -0.22, 0.18) if cuts else 1.0
    values = jax.random.normal(rng, shape, jnp.float32) * scale * factor_of
    return jnp.minimum(jnp.maximum(values, -reach), reach).astype(held_as)


def setup_inputs(seed: int = 0) -> dict:
    arg_keys = jax.random.split(jax.random.key(seed), 6)
    return {
        "right_sides": gaussian(arg_keys[0], (LAYERS, 2, SHOTS, PLANE), 1.0, 6.0, ((0, 8), (3, 4))),
        "sources": plant(jax.random.randint(arg_keys[1], (SHOTS,), 0, PLANE), jax.random.fold_in(arg_keys[1], 1), 0, PLANE - 1).astype(jnp.int32),
        "coupling": draw_coupling(jax.random.fold_in(arg_keys[5], 71), 0),
        "block_cols": draw_block_cols(jax.random.fold_in(arg_keys[5], 71), 0),
        "factors": draw_factors(jax.random.fold_in(arg_keys[5], 71), 0),
    }


source_gain = 8.0


def apply_whole(vector, columns, factor_set):
    shot_count = vector.shape[1]
    padding = REACH * BLOCK
    extended = jnp.pad(vector.astype(jnp.float32), ((0, 0), (0, 0), (padding, padding)))
    pieces = extended.reshape(2, shot_count, -1, BLOCK)
    index = (columns + REACH).reshape(-1).astype(jnp.int32)
    picked = jnp.take(pieces, index, axis=2).reshape(2, shot_count, NBLK, NNZ, BLOCK)
    product = jnp.einsum("psrnj,rnqji->pqsri", picked, factor_set.astype(jnp.float32), precision=lax.Precision.HIGHEST)
    real_part = product[0, 0] - product[1, 1]
    imag_part = product[0, 1] + product[1, 0]
    return jnp.stack([real_part, imag_part]).reshape(2, shot_count, PLANE)


def reference(right_sides, sources, coupling, block_cols, factors):
    spike = jnp.zeros((SHOTS, PLANE), jnp.float32).at[jnp.arange(SHOTS), sources].set(source_gain)

    def down_step(previous, items):
        layer_rhs, couple_row, columns, factor_set = items
        source_load = layer_rhs.astype(jnp.float32)
        source_load = source_load.at[0].add(spike)
        mixed_in = (source_load - couple_row[None, None, :] * previous.astype(jnp.float32)).astype(jnp.bfloat16)
        result = apply_whole(mixed_in, columns, factor_set).astype(jnp.bfloat16)
        return result, result

    start = jnp.zeros((2, SHOTS, PLANE), jnp.bfloat16)
    _, stored = lax.scan(down_step, start, (right_sides, coupling, block_cols, factors))

    def up_step(carried, items):
        down_field, couple_row, columns, factor_set = items
        updated = (down_field.astype(jnp.float32) - apply_whole(carried, columns, factor_set)).astype(jnp.bfloat16)
        handed = (couple_row[None, None, :] * updated.astype(jnp.float32)).astype(jnp.bfloat16)
        return handed, updated

    _, solution = lax.scan(up_step, start, (stored, coupling, block_cols, factors), reverse=True)
    return solution
```

```python
import functools

import jax
import jax.numpy as jnp
from jax import lax
from jax.experimental import pallas as pl
from jax.experimental.pallas import tpu as pltpu
from jax.sharding import PartitionSpec as P

REACH = 3
DEEP = 2 * REACH
FRONTS = 4
SHALLOW = 2

source_gain = 8.0

MESH = pl.DeviceIdType.MESH


def sweep_kernel(
    depth_count, lat_count, fronts,
    srcs_ref, cols_ref, rhs_ref, coup_ref, fac_ref, out_ref,
    ext, near, din, uin, dmid, whalo, wa, wb, mixed, hout, rbuf, cbuf, facs, obuf, spread, kvec, kcols,
    d_send, d_recv, u_send, u_recv, m_send, m_recv, w_send, w_recv, p_send, p_recv, o_send, o_recv, k_sem, go_sem,
):
    d = lax.axis_index("depth")
    l = lax.axis_index("lat")
    tile, stored, _, blk, _ = fac_ref.shape[1:]
    shot_count = rhs_ref.shape[2]
    shots = shot_count // fronts
    own = 2 * tile
    total_rows = own + 2 * DEEP
    chips = lat_count // 2
    chip = l // 2
    odd = lax.rem(l, 2)
    worker = odd == 1
    flip = chip // (chips - 1)
    interior = (chip > 0) & (chip < chips - 1)
    shallow = d < SHALLOW
    early = d >= depth_count // 2
    deepest = d == depth_count - 1
    bf16, f32 = jnp.bfloat16, jnp.float32

    def mirrored(a, b):
        return a + flip * (b - a)

    def e_of(q):
        return mirrored(q + DEEP, own - 1 - q + DEEP)

    def r_of(q):
        return mirrored(q, own - 1 - q)

    def place(q):
        a, b = q + DEEP, own - 1 - q + DEEP
        return mirrored(a // tile, b // tile), mirrored(a % tile, b % tile)

    def lanes(i):
        return pl.ds(pl.multiple_of(i * blk, blk), blk)

    def front_of(f):
        return pl.ds(pl.multiple_of(f * shots, shots), shots)

    def remote(src, dst, ssem, rsem, dd, to_l):
        return pltpu.make_async_remote_copy(
            src_ref=src, dst_ref=dst, send_sem=ssem, recv_sem=rsem,
            device_id=(d + dd, to_l), device_id_type=MESH,
        )

    def parts_of(which, slot, halo):
        if which == 0:
            return cols_ref, kvec.at[slot]
        if which == 1:
            return coup_ref, cbuf.at[slot]
        if which == 2:
            return rhs_ref.at[0], rbuf.at[slot, 0]
        if which == 3 and halo:
            place_ = pl.ds(pl.multiple_of(odd * (tile - REACH) * blk, blk), REACH * blk)
            return rhs_ref.at[1, :, :, place_], rbuf.at[slot, 1, :, :, place_]
        if which == 3:
            return rhs_ref.at[1], rbuf.at[slot, 1]
        layer = which - 4
        if halo:
            first = (1 - odd) * (own + REACH)
            return fac_ref.at[layer, pl.ds(odd * (tile - REACH), REACH)], facs.at[layer, pl.ds(first, REACH)]
        return fac_ref.at[layer], facs.at[layer, pl.ds(REACH + (slot - 1) * tile, tile)]

    def home_copy(which):
        src, dst = parts_of(which, 1, False)
        return remote(src, dst, p_send.at[0, which], p_recv.at[1, which], 0, l + 1)

    def halo_copy(which):
        slot = 3 * (1 - odd)
        src, dst = parts_of(which, slot, True)
        return remote(src, dst, p_send.at[1, which], p_recv.at[slot, which], 0, l - 1 + 3 * odd)

    def halo_arrival(which, high):
        slot = 3 * high
        if which == 3:
            place_ = pl.ds(pl.multiple_of((1 - high) * (tile - REACH) * blk, blk), REACH * blk)
            src, dst = rhs_ref.at[1, :, :, place_], rbuf.at[slot, 1, :, :, place_]
        elif which > 3:
            src = fac_ref.at[which - 4, pl.ds(0, REACH)]
            dst = facs.at[which - 4, pl.ds(high * (own + REACH), REACH)]
        else:
            src, dst = parts_of(which, slot, True)
        return remote(src, dst, p_send.at[1, which], p_recv.at[slot, which], 0, l - 1)

    halo_ok = (l > 0) & (l < lat_count - 1)

    def own_copy(which):
        if which == 0:
            return pltpu.make_async_copy(cols_ref, kcols.at[2], p_recv.at[2, 0])
        src, dst = parts_of(which, 2, False)
        return pltpu.make_async_copy(src, dst, p_recv.at[2, which])

    @pl.when(worker)
    def _():
        for which in range(6):
            own_copy(which).start()

    barrier = pltpu.get_barrier_semaphore()
    total = jnp.int32(0)
    for dd, dl in [(0, -1), (0, 1)] + [(a, b) for a in (-1, 0, 1) for b in (-2, 0, 2) if (a, b) != (0, 0)]:
        ok = (d + dd >= 0) & (d + dd < depth_count) & (l + dl >= 0) & (l + dl < lat_count)
        if dl in (-2, 0, 2):
            ok = ok & worker

        @pl.when(ok)
        def _():
            pl.semaphore_signal(barrier, inc=1, device_id=(d + dd, l + dl), device_id_type=MESH)

        total = total + ok.astype(jnp.int32)

    for shot in range(shot_count):
        spread[pl.ds(shot, 1), :] = jnp.full((1, blk), srcs_ref[shot], jnp.int32)

    pl.semaphore_wait(barrier, total)

    def halo_start(which, also):
        @pl.when(halo_ok & also)
        def _():
            halo_copy(which).start()

    def out_copy(f):
        front = front_of(f)
        return remote(
            obuf.at[0, :, :, front], out_ref.at[:, :, front], o_send.at[f], o_recv.at[f], 0, l - 1 + 2 * (1 - odd)
        )

    def out_local(f):
        front = front_of(f)
        return pltpu.make_async_copy(obuf.at[1, :, :, front], out_ref.at[:, :, front], o_recv.at[f])

    @pl.when(jnp.logical_not(worker))
    def _():
        for which in range(6):
            home_copy(which).start()

    always = d >= 0
    for which in range(3):
        halo_start(which, always)
    for which in (3, 4):
        halo_start(which, jnp.logical_not(shallow))
    halo_start(5, early)

    @pl.when(jnp.logical_not(worker))
    def _():
        @pl.when(jnp.logical_not(early))
        def _():
            pl.semaphore_wait(go_sem, 1)

        halo_start(5, jnp.logical_not(early))
        for which in range(6):
            home_copy(which).wait_send()

        @pl.loop(0, fronts)
        def _(f):
            out_copy(f).wait_recv()

    first_row = chip * own
    lane = lax.broadcasted_iota(jnp.int32, (shots, blk), 1)
    first_cell = (first_row - DEEP) * blk

    def load_of(layer, f, q):
        t, i = place(q)
        front = front_of(f)
        spike = jnp.where(spread[front, :] == first_cell + e_of(q) * blk + lane, source_gain, 0.0).astype(f32)
        real = rbuf[t, layer, 0, front, lanes(i)].astype(f32) + spike
        imag = rbuf[t, layer, 1, front, lanes(i)].astype(f32)
        return jnp.concatenate([real, imag], axis=0)

    def coup_of(layer, q):
        t, i = place(q)
        return cbuf[t, pl.ds(layer, 1), lanes(i)]

    def apply_row(layer, q, field, shift):
        t, i = place(q)
        top = field.shape[0] - 1
        xs = [
            field[jnp.clip(kcols[t, layer, i * stored + n] - first_row + shift, 0, top)] for n in range(stored)
        ]
        x = jnp.concatenate(xs, axis=1)
        row = e_of(q) - (DEEP - REACH)
        w = jnp.concatenate(
            [jnp.concatenate([facs[layer, row, n, 0], facs[layer, row, n, 1]], axis=1) for n in range(stored)],
            axis=0,
        )
        p = jnp.dot(x, w, preferred_element_type=f32)
        real = p[:shots, :blk] - p[shots:, blk:]
        imag = p[:shots, blk:] + p[shots:, :blk]
        return jnp.concatenate([real, imag], axis=0)

    last_l = l + 2 - 4 * flip

    chunks = ((0, DEEP), (own - DEEP, REACH), (own - REACH, REACH))

    def own_chunk(f, k, src, dst, ssem, rsem, dd):
        a, n = chunks[k]
        r0 = mirrored(a, own - a - n)
        return remote(
            src.at[f, pl.ds(r0, n)], dst.at[f, pl.ds(r0 + DEEP, n)], ssem.at[f, k], rsem.at[f, k], dd, l
        )

    def cross_chunk(f, j, src, dst, ssem, rsem, dd):
        a, n = chunks[1 + j]
        r0 = mirrored(a, own - a - n)
        e0 = mirrored(a - own + DEEP, own - a - n + own + DEEP)
        return remote(
            src.at[f, pl.ds(r0, n)], dst.at[f, pl.ds(e0, n)],
            ssem.at[f, 3 + j], rsem.at[f, 3 + 2 * flip + j], dd, last_l,
        )

    def back_chunk(f, j, src, dst, ssem, rsem, dd):
        r0 = REACH * (1 - j)
        return remote(
            src.at[f, pl.ds(r0, REACH)], dst.at[f, pl.ds(r0 + own + DEEP, REACH)],
            ssem.at[f, 5 + j], rsem.at[f, 5 + j], dd, l - 2,
        )

    def wait_chunk(f, slot, e0, n, dst, src, ssem, rsem, dd):
        remote(
            src.at[f, pl.ds(0, n)], dst.at[f, pl.ds(e0, n)], ssem.at[f, 0], rsem.at[f, slot], dd, l
        ).wait_recv()

    def wait_own(f, k, dst, src, ssem, rsem, dd):
        a, n = chunks[k]
        wait_chunk(f, k, DEEP + mirrored(a, own - a - n), n, dst, src, ssem, rsem, dd)

    def wait_cross(f, j, dst, src, ssem, rsem, dd):
        q0 = own + DEEP - REACH * (1 + j)
        e0 = mirrored(q0 + DEEP, own - q0 - REACH + DEEP)
        wait_chunk(f, 5 - 2 * flip + j, e0, REACH, dst, src, ssem, rsem, dd)

    def wait_back(f, j, dst, src, ssem, rsem, dd):
        wait_chunk(f, 3 + j, REACH * j, REACH, dst, src, ssem, rsem, dd)

    def depth_start(f, q, src, dst, ssem, rsem, dd):
        ks = [k for k in (2, 1, 0) if chunks[k][0] == q]
        if not ks:
            return
        k = ks[0]
        args = (src, dst, ssem, rsem, dd)

        @pl.when((d + dd >= 0) & (d + dd < depth_count))
        def _():
            if k > 0:
                cross_chunk(f, k - 1, *args).start()
            own_chunk(f, k, *args).start()
            if k == 0:
                @pl.when(interior)
                def _():
                    back_chunk(f, 0, *args).start()
                    back_chunk(f, 1, *args).start()

    def depth_sent(f, src, dst, ssem, rsem, dd):
        args = (src, dst, ssem, rsem, dd)

        @pl.when((d + dd >= 0) & (d + dd < depth_count))
        def _():
            for k in range(3):
                own_chunk(f, k, *args).wait_send()
            for j in range(2):
                cross_chunk(f, j, *args).wait_send()

            @pl.when(interior)
            def _():
                for j in range(2):
                    back_chunk(f, j, *args).wait_send()

    def wait_inbound(f, args):
        for k in range(3):
            wait_own(f, k, *args)
        for j in range(2):
            wait_cross(f, j, *args)

    def side_copy(f, src, dst, ssem, rsem):
        r0 = mirrored(own - REACH, 0)
        return remote(src.at[f, pl.ds(r0, REACH)], dst.at[f, flip], ssem.at[f, 0], rsem.at[f, flip], 0, last_l)

    def side_back(f, src, dst, ssem, rsem):
        return remote(src.at[f, pl.ds(0, REACH)], dst.at[f, 1], ssem.at[f, 1], rsem.at[f, 1], 0, l - 2)

    def side_start(f, *args):
        side_copy(f, *args).start()

        @pl.when(interior)
        def _():
            side_back(f, *args).start()

    def side_sent(f, *args):
        side_copy(f, *args).wait_send()

        @pl.when(interior)
        def _():
            side_back(f, *args).wait_send()

    def side_wait(f, side, src, dst, ssem, rsem):
        remote(
            src.at[f, pl.ds(0, REACH)], dst.at[f, side], ssem.at[f, 0], rsem.at[f, side], 0, last_l
        ).wait_recv()

    mid = (mixed, dmid, m_send, m_recv)
    wside = (wb, whalo, w_send, w_recv)
    down_in = (din, wb, d_send, d_recv, -1)
    down_out = (wb, din, d_send, d_recv, 1)
    up_in = (uin, hout, u_send, u_recv, 1)
    up_out = (hout, uin, u_send, u_recv, -1)

    def halo_row(q):
        return mirrored(q - own, own + REACH - 1 - q)

    def put(f, q):
        e = e_of(q)
        previous = jnp.where(d > 0, din[f, e].astype(f32), 0.0)
        ext[e] = (load_of(0, f, q) - coup_of(0, q) * previous).astype(bf16)

    def first_layer(f, q):
        w = apply_row(0, q, ext, DEEP).astype(bf16)
        return w, (load_of(1, f, q) - coup_of(1, q) * w.astype(f32)).astype(bf16)

    def second_layer(f):
        for q in reversed(range(own)):
            wb[f, r_of(q)] = apply_row(1, q, near, REACH).astype(bf16)
            depth_start(f, q, *down_out)
        side_start(f, *wside)

    def down_shallow_first(f):
        @pl.when(d > 0)
        def _():
            wait_inbound(f, down_in)

        @pl.when(interior)
        def _():
            @pl.when(d > 0)
            def _():
                for j in range(2):
                    wait_back(f, j, *down_in)
            for q in range(-DEEP, 0):
                put(f, q)

        for q in range(own + DEEP):
            put(f, q)
        for q in reversed(range(own)):
            w, g = first_layer(f, q)
            wa[f, r_of(q)] = w
            mixed[f, r_of(q)] = g
            if q == own - REACH:
                side_copy(f, *mid).start()

        @pl.when(interior)
        def _():
            side_back(f, *mid).start()

    def down_shallow_second(f):
        for r in range(own):
            near[REACH + r] = mixed[f, r]
        side_wait(f, 1 - flip, *mid)
        for q in range(own, own + REACH):
            near[e_of(q) - REACH] = dmid[f, 1 - flip, halo_row(q)]

        @pl.when(interior)
        def _():
            side_wait(f, 0, *mid)
            for i in range(REACH):
                near[i] = dmid[f, 0, i]

        second_layer(f)

    def down_deep(f):
        wait_inbound(f, down_in)
        for q in range(own + DEEP):
            put(f, q)

        @pl.when(interior)
        def _():
            for j in range(2):
                wait_back(f, j, *down_in)
            for q in range(-DEEP, 0):
                put(f, q)
            for q in range(-REACH, 0):
                near[e_of(q) - REACH] = first_layer(f, q)[1]

        for q in range(own + REACH):
            w, g = first_layer(f, q)
            if q < own:
                wa[f, r_of(q)] = w
            near[e_of(q) - REACH] = g
        second_layer(f)

    def emit(layer, f, q, value):
        s = value.astype(bf16)
        t, i = place(q)
        front = front_of(f)
        obuf[t - 1, layer, 0, front, lanes(i)] = s[:shots]
        obuf[t - 1, layer, 1, front, lanes(i)] = s[shots:]
        return (coup_of(layer, q) * s.astype(f32)).astype(bf16)

    def coupled(q, value):
        return (coup_of(1, q) * value.astype(bf16).astype(f32)).astype(bf16)

    def finish(f):
        for q in reversed(range(own)):
            r = r_of(q)
            hout[f, r] = emit(0, f, q, wa[f, r].astype(f32) - apply_row(0, q, near, REACH))
            depth_start(f, q, *up_out)
        out_copy(f).start()
        out_local(f).start()

    def up_last(f):
        side_wait(f, 1 - flip, *wside)
        for q in range(own):
            near[e_of(q) - REACH] = emit(1, f, q, wb[f, r_of(q)].astype(f32))
        for q in range(own, own + REACH):
            near[e_of(q) - REACH] = coupled(q, whalo[f, 1 - flip, halo_row(q)].astype(f32))

        @pl.when(interior)
        def _():
            side_wait(f, 0, *wside)
            for i in range(REACH):
                near[i] = coupled(i - REACH, whalo[f, 0, i].astype(f32))

        finish(f)

    def up(f):
        side_wait(f, 1 - flip, *wside)
        wait_inbound(f, up_in)
        for q in range(own + DEEP):
            ext[e_of(q)] = uin[f, e_of(q)]

        @pl.when(interior)
        def _():
            side_wait(f, 0, *wside)
            for j in range(2):
                wait_back(f, j, *up_in)
            for q in range(-DEEP, 0):
                ext[e_of(q)] = uin[f, e_of(q)]
            for q in range(-REACH, 0):
                value = whalo[f, 0, q + REACH].astype(f32) - apply_row(1, q, ext, DEEP)
                near[e_of(q) - REACH] = coupled(q, value)

        for q in range(own + REACH):
            part = apply_row(1, q, ext, DEEP)
            if q < own:
                near[e_of(q) - REACH] = emit(1, f, q, wb[f, r_of(q)].astype(f32) - part)
            else:
                near[e_of(q) - REACH] = coupled(q, whalo[f, 1 - flip, halo_row(q)].astype(f32) - part)
        finish(f)

    def table_local(slot):
        return pltpu.make_async_copy(kvec.at[slot], kcols.at[slot], k_sem)

    def home_wait(which):
        own_copy(which).wait()
        home_copy(which).wait_recv()
        if which == 0:
            table_local(1).start()
            table_local(1).wait()

    def halo_wait(which):
        slot = 3 * (1 - flip)
        halo_arrival(which, 1 - flip).wait_recv()
        if which == 0:
            table_local(slot).start()
            table_local(slot).wait()

        @pl.when(interior)
        def _():
            halo_arrival(which, 0).wait_recv()
            if which == 0:
                table_local(0).start()
                table_local(0).wait()

    @pl.when(worker)
    def _():
        for which in range(3):
            halo_wait(which)
        for which in range(5):
            home_wait(which)

        @pl.when(shallow)
        def _():
            @pl.loop(0, fronts + 1)
            def _(t):
                @pl.when(t < fronts)
                def _():
                    down_shallow_first(t)

                @pl.when(t == 0)
                def _():
                    home_wait(5)

                @pl.when(t > 0)
                def _():
                    down_shallow_second(t - 1)

        @pl.when(jnp.logical_not(shallow))
        def _():
            home_wait(5)
            for which in (3, 4):
                halo_wait(which)

            @pl.loop(0, fronts)
            def _(f):
                down_deep(f)

                @pl.when(deepest & (f > 0))
                def _():
                    up_last(f - 1)

        @pl.when(jnp.logical_not(early))
        def _():
            pl.semaphore_signal(go_sem, inc=1, device_id=(d, l - 1), device_id_type=MESH)

        halo_start(5, jnp.logical_not(early))
        halo_wait(5)

        @pl.when(deepest)
        def _():
            up_last(fronts - 1)

        @pl.when(jnp.logical_not(deepest))
        def _():
            @pl.loop(0, fronts)
            def _(f):
                up(f)

        @pl.loop(0, fronts)
        def _(f):
            @pl.when(shallow)
            def _():
                side_sent(f, *mid)

            side_sent(f, *wside)
            depth_sent(f, *down_out)
            depth_sent(f, *up_out)
            out_copy(f).wait_send()
            out_local(f).wait()

    for which in range(6):
        @pl.when(halo_ok & jnp.logical_not(shallow) if which in (3, 4) else halo_ok)
        def _():
            halo_copy(which).wait_send()


def per_device(right_sides, sources, coupling, block_cols, factors):
    layers, parts, shot_count, cells = right_sides.shape
    rows, stored = block_cols.shape[1:]
    blk = factors.shape[-1]
    lat_count = lax.axis_size("lat")
    assert lax.axis_size("depth") > SHALLOW and layers == 2 and rows == DEEP and parts == 2
    assert lat_count % 2 == 0 and lat_count >= 4
    fronts = FRONTS
    pair = parts * (shot_count // fronts)
    own = 2 * rows
    ext_rows = own + 2 * DEEP
    bf16 = jnp.bfloat16
    table = block_cols.reshape(layers, rows * stored)
    table = jnp.pad(table, ((0, 8 - layers), (0, 128 - rows * stored)))
    anywhere = pl.BlockSpec(memory_space=pl.ANY)
    vmem = pl.BlockSpec(memory_space=pltpu.VMEM)
    smem = pl.BlockSpec(memory_space=pltpu.SMEM)
    dma = pltpu.SemaphoreType.DMA
    return pl.pallas_call(
        functools.partial(sweep_kernel, lax.axis_size("depth"), lat_count, fronts),
        out_shape=jax.ShapeDtypeStruct(right_sides.shape, bf16),
        in_specs=[smem, vmem, anywhere, anywhere, anywhere],
        out_specs=anywhere,
        scratch_shapes=[
            pltpu.VMEM((ext_rows, pair, blk), bf16),
            pltpu.VMEM((own + 2 * REACH, pair, blk), bf16),
            pltpu.VMEM((fronts, ext_rows, pair, blk), bf16),
            pltpu.VMEM((fronts, ext_rows, pair, blk), bf16),
            pltpu.VMEM((fronts, 2, REACH, pair, blk), bf16),
            pltpu.VMEM((fronts, 2, REACH, pair, blk), bf16),
            pltpu.VMEM((fronts, own, pair, blk), bf16),
            pltpu.VMEM((fronts, own, pair, blk), bf16),
            pltpu.VMEM((fronts, own, pair, blk), bf16),
            pltpu.VMEM((fronts, own, pair, blk), bf16),
            pltpu.VMEM((4,) + right_sides.shape, bf16),
            pltpu.VMEM((4,) + coupling.shape, jnp.float32),
            pltpu.VMEM((layers, own + 2 * REACH) + factors.shape[2:], bf16),
            pltpu.VMEM((2,) + right_sides.shape, bf16),
            pltpu.VMEM((shot_count, blk), jnp.int32),
            pltpu.VMEM((4,) + table.shape, jnp.int32),
            pltpu.SMEM((4,) + table.shape, jnp.int32),
            dma((fronts, 7)), dma((fronts, 7)), dma((fronts, 7)), dma((fronts, 7)),
            dma((fronts, 2)), dma((fronts, 2)), dma((fronts, 2)), dma((fronts, 2)),
            dma((2, 6)), dma((4, 6)), dma((fronts,)), dma((fronts,)), dma, pltpu.SemaphoreType.REGULAR,
        ],
        compiler_params=pltpu.CompilerParams(
            collective_id=0, has_side_effects=True, vmem_limit_bytes=40 * 2**20
        ),
    )(sources, table, right_sides, coupling, factors)


def solution(mesh):
    in_specs = (
        P("depth", None, None, "lat"),
        P(),
        P("depth", "lat"),
        P("depth", "lat", None),
        P("depth", "lat", None, None, None, None),
    )
    out_specs = P("depth", None, None, "lat")
    return jax.shard_map(
        per_device, mesh=mesh, in_specs=in_specs, out_specs=out_specs, check_vma=False
    )
```

```python
import functools

import jax
import jax.numpy as jnp
from jax import lax
from jax.experimental import pallas as pl
from jax.experimental.pallas import tpu as pltpu
from jax.sharding import PartitionSpec as P

REACH = 3
DEEP = 2 * REACH
FRONTS = 4
SHALLOW = 2

source_gain = 8.0

MESH = pl.DeviceIdType.MESH


def sweep_kernel(
    depth_count, lat_count, fronts,
    srcs_ref, cols_ref, rhs_ref, coup_ref, fac_ref, out_ref,
    ext, near, din, uin, dmid, whalo, wa, wb, mixed, hout, rbuf, cbuf, facs, obuf, spread, kvec, kcols,
    d_send, d_recv, u_send, u_recv, m_send, m_recv, w_send, w_recv, p_send, p_recv, o_send, o_recv, k_sem, go_sem,
):
    d = lax.axis_index("depth")
    l = lax.axis_index("lat")
    tile, stored, _, blk, _ = fac_ref.shape[1:]
    shot_count = rhs_ref.shape[2]
    shots = shot_count // fronts
    own = 2 * tile
    total_rows = own + 2 * DEEP
    chips = lat_count // 2
    chip = l // 2
    odd = lax.rem(l, 2)
    worker = odd == 1
    flip = chip // (chips - 1)
    interior = (chip > 0) & (chip < chips - 1)
    shallow = d < SHALLOW
    early = d >= depth_count // 2
    deepest = d == depth_count - 1
    bf16, f32 = jnp.bfloat16, jnp.float32

    def mirrored(a, b):
        return a + flip * (b - a)

    def e_of(q):
        return mirrored(q + DEEP, own - 1 - q + DEEP)

    def r_of(q):
        return mirrored(q, own - 1 - q)

    def place(q):
        a, b = q + DEEP, own - 1 - q + DEEP
        return mirrored(a // tile, b // tile), mirrored(a % tile, b % tile)

    def lanes(i):
        return pl.ds(pl.multiple_of(i * blk, blk), blk)

    def front_of(f):
        return pl.ds(pl.multiple_of(f * shots, shots), shots)

    def remote(src, dst, ssem, rsem, dd, to_l):
        return pltpu.make_async_remote_copy(
            src_ref=src, dst_ref=dst, send_sem=ssem, recv_sem=rsem,
            device_id=(d + dd, to_l), device_id_type=MESH,
        )

    def parts_of(which, slot, halo):
        if which == 0:
            return cols_ref, kvec.at[slot]
        if which == 1:
            return coup_ref, cbuf.at[slot]
        if which == 2:
            return rhs_ref.at[0], rbuf.at[slot, 0]
        if which == 3 and halo:
            place_ = pl.ds(pl.multiple_of(odd * (tile - REACH) * blk, blk), REACH * blk)
            return rhs_ref.at[1, :, :, place_], rbuf.at[slot, 1, :, :, place_]
        if which == 3:
            return rhs_ref.at[1], rbuf.at[slot, 1]
        layer = which - 4
        if halo:
            first = (1 - odd) * (own + REACH)
            return fac_ref.at[layer, pl.ds(odd * (tile - REACH), REACH)], facs.at[layer, pl.ds(first, REACH)]
        return fac_ref.at[layer], facs.at[layer, pl.ds(REACH + (slot - 1) * tile, tile)]

    def home_copy(which):
        src, dst = parts_of(which, 1, False)
        return remote(src, dst, p_send.at[0, which], p_recv.at[1, which], 0, l + 1)

    def halo_copy(which):
        slot = 3 * (1 - odd)
        src, dst = parts_of(which, slot, True)
        return remote(src, dst, p_send.at[1, which], p_recv.at[slot, which], 0, l - 1 + 3 * odd)

    def halo_arrival(which, high):
        slot = 3 * high
        if which == 3:
            place_ = pl.ds(pl.multiple_of((1 - high) * (tile - REACH) * blk, blk), REACH * blk)
            src, dst = rhs_ref.at[1, :, :, place_], rbuf.at[slot, 1, :, :, place_]
        elif which > 3:
            src = fac_ref.at[which - 4, pl.ds(0, REACH)]
            dst = facs.at[which - 4, pl.ds(high * (own + REACH), REACH)]
        else:
            src, dst = parts_of(which, slot, True)
        return remote(src, dst, p_send.at[1, which], p_recv.at[slot, which], 0, l - 1)

    halo_ok = (l > 0) & (l < lat_count - 1)

    def own_copy(which):
        if which == 0:
            return pltpu.make_async_copy(cols_ref, kcols.at[2], p_recv.at[2, 0])
        src, dst = parts_of(which, 2, False)
        return pltpu.make_async_copy(src, dst, p_recv.at[2, which])

    @pl.when(worker)
    def _():
        for which in range(6):
            own_copy(which).start()

    barrier = pltpu.get_barrier_semaphore()
    total = jnp.int32(0)
    for dd, dl in [(0, -1), (0, 1)] + [(a, b) for a in (-1, 0, 1) for b in (-2, 0, 2) if (a, b) != (0, 0)]:
        ok = (d + dd >= 0) & (d + dd < depth_count) & (l + dl >= 0) & (l + dl < lat_count)
        if dl in (-2, 0, 2):
            ok = ok & worker

        @pl.when(ok)
        def _():
            pl.semaphore_signal(barrier, inc=1, device_id=(d + dd, l + dl), device_id_type=MESH)

        total = total + ok.astype(jnp.int32)

    for shot in range(shot_count):
        spread[pl.ds(shot, 1), :] = jnp.full((1, blk), srcs_ref[shot], jnp.int32)

    pl.semaphore_wait(barrier, total)

    def halo_start(which, also):
        @pl.when(halo_ok & also)
        def _():
            halo_copy(which).start()

    def out_copy(f):
        front = front_of(f)
        return remote(
            obuf.at[0, :, :, front], out_ref.at[:, :, front], o_send.at[f], o_recv.at[f], 0, l - 1 + 2 * (1 - odd)
        )

    def out_local(f):
        front = front_of(f)
        return pltpu.make_async_copy(obuf.at[1, :, :, front], out_ref.at[:, :, front], o_recv.at[f])

    @pl.when(jnp.logical_not(worker))
    def _():
        for which in range(6):
            home_copy(which).start()

    always = d >= 0
    for which in range(3):
        halo_start(which, always)
    for which in (3, 4):
        halo_start(which, jnp.logical_not(shallow))
    halo_start(5, early)

    @pl.when(jnp.logical_not(worker))
    def _():
        @pl.when(jnp.logical_not(early))
        def _():
            pl.semaphore_wait(go_sem, 1)

        halo_start(5, jnp.logical_not(early))
        for which in range(6):
            home_copy(which).wait_send()

        @pl.loop(0, fronts)
        def _(f):
            out_copy(f).wait_recv()

    first_row = chip * own
    lane = lax.broadcasted_iota(jnp.int32, (shots, blk), 1)
    first_cell = (first_row - DEEP) * blk

    def load_of(layer, f, q):
        t, i = place(q)
        front = front_of(f)
        spike = jnp.where(spread[front, :] == first_cell + e_of(q) * blk + lane, source_gain, 0.0).astype(f32)
        real = rbuf[t, layer, 0, front, lanes(i)].astype(f32) + spike
        imag = rbuf[t, layer, 1, front, lanes(i)].astype(f32)
        return jnp.concatenate([real, imag], axis=0)

    def coup_of(layer, q):
        t, i = place(q)
        return cbuf[t, pl.ds(layer, 1), lanes(i)]

    def apply_row(layer, q, field, shift):
        t, i = place(q)
        top = field.shape[0] - 1
        xs = [
            field[jnp.clip(kcols[t, layer, i * stored + n] - first_row + shift, 0, top)] for n in range(stored)
        ]
        x = jnp.concatenate(xs, axis=1)
        row = e_of(q) - (DEEP - REACH)
        w = jnp.concatenate(
            [jnp.concatenate([facs[layer, row, n, 0], facs[layer, row, n, 1]], axis=1) for n in range(stored)],
            axis=0,
        )
        p = jnp.dot(x, w, preferred_element_type=f32)
        real = p[:shots, :blk] - p[shots:, blk:]
        imag = p[:shots, blk:] + p[shots:, :blk]
        return jnp.concatenate([real, imag], axis=0)

    last_l = l + 2 - 4 * flip

    own_chunks = own // REACH
    cross_first = own_chunks - DEEP // REACH

    def own_chunk(f, k, src, dst, ssem, rsem, dd):
        a, n = k * REACH, REACH
        r0 = mirrored(a, own - a - n)
        return remote(
            src.at[f, pl.ds(r0, n)], dst.at[f, pl.ds(r0 + DEEP, n)], ssem.at[f, k], rsem.at[f, k], dd, l
        )

    def cross_chunk(f, j, src, dst, ssem, rsem, dd):
        a, n = (cross_first + j) * REACH, REACH
        r0 = mirrored(a, own - a - n)
        e0 = mirrored(a - own + DEEP, own - a - n + own + DEEP)
        return remote(
            src.at[f, pl.ds(r0, n)], dst.at[f, pl.ds(e0, n)],
            ssem.at[f, own_chunks + j], rsem.at[f, own_chunks + 2 * flip + j], dd, last_l,
        )

    def back_chunk(f, j, src, dst, ssem, rsem, dd):
        r0 = REACH * (1 - j)
        return remote(
            src.at[f, pl.ds(r0, REACH)], dst.at[f, pl.ds(r0 + own + DEEP, REACH)],
            ssem.at[f, own_chunks + 2 + j], rsem.at[f, own_chunks + 2 + j], dd, l - 2,
        )

    def wait_chunk(f, slot, e0, n, dst, src, ssem, rsem, dd):
        remote(
            src.at[f, pl.ds(0, n)], dst.at[f, pl.ds(e0, n)], ssem.at[f, 0], rsem.at[f, slot], dd, l
        ).wait_recv()

    def wait_own(f, k, dst, src, ssem, rsem, dd):
        a, n = k * REACH, REACH
        wait_chunk(f, k, DEEP + mirrored(a, own - a - n), n, dst, src, ssem, rsem, dd)

    def wait_cross(f, j, dst, src, ssem, rsem, dd):
        q0 = own + DEEP - REACH * (1 + j)
        e0 = mirrored(q0 + DEEP, own - q0 - REACH + DEEP)
        wait_chunk(f, own_chunks + 2 - 2 * flip + j, e0, REACH, dst, src, ssem, rsem, dd)

    def wait_back(f, j, dst, src, ssem, rsem, dd):
        wait_chunk(f, own_chunks + j, REACH * j, REACH, dst, src, ssem, rsem, dd)

    def depth_start(f, k, src, dst, ssem, rsem, dd):
        args = (src, dst, ssem, rsem, dd)

        @pl.when((d + dd >= 0) & (d + dd < depth_count))
        def _():
            if k >= cross_first:
                cross_chunk(f, k - cross_first, *args).start()
            own_chunk(f, k, *args).start()
            if k == 1:
                @pl.when(interior)
                def _():
                    back_chunk(f, 0, *args).start()
                    back_chunk(f, 1, *args).start()

    def depth_sent(f, src, dst, ssem, rsem, dd):
        args = (src, dst, ssem, rsem, dd)

        @pl.when((d + dd >= 0) & (d + dd < depth_count))
        def _():
            for k in range(own_chunks):
                own_chunk(f, k, *args).wait_send()
            for j in range(2):
                cross_chunk(f, j, *args).wait_send()

            @pl.when(interior)
            def _():
                for j in range(2):
                    back_chunk(f, j, *args).wait_send()

    def wait_inbound(f, args):
        for k in range(own_chunks):
            wait_own(f, k, *args)
        for j in range(2):
            wait_cross(f, j, *args)

    def side_copy(f, src, dst, ssem, rsem):
        r0 = mirrored(own - REACH, 0)
        return remote(src.at[f, pl.ds(r0, REACH)], dst.at[f, flip], ssem.at[f, 0], rsem.at[f, flip], 0, last_l)

    def side_back(f, src, dst, ssem, rsem):
        return remote(src.at[f, pl.ds(0, REACH)], dst.at[f, 1], ssem.at[f, 1], rsem.at[f, 1], 0, l - 2)

    def side_start(f, *args):
        side_copy(f, *args).start()

        @pl.when(interior)
        def _():
            side_back(f, *args).start()

    def side_sent(f, *args):
        side_copy(f, *args).wait_send()

        @pl.when(interior)
        def _():
            side_back(f, *args).wait_send()

    def side_wait(f, side, src, dst, ssem, rsem):
        remote(
            src.at[f, pl.ds(0, REACH)], dst.at[f, side], ssem.at[f, 0], rsem.at[f, side], 0, last_l
        ).wait_recv()

    mid = (mixed, dmid, m_send, m_recv)
    wside = (wb, whalo, w_send, w_recv)
    down_in = (din, wb, d_send, d_recv, -1)
    down_out = (wb, din, d_send, d_recv, 1)
    up_in = (uin, hout, u_send, u_recv, 1)
    up_out = (hout, uin, u_send, u_recv, -1)

    def rows_of(k):
        return range(k * REACH, (k + 1) * REACH)

    def wave(f, inbound, outbound, take, take_back, first, second):
        for k in range(own_chunks):
            wait_own(f, k, *inbound)
            for q in rows_of(k):
                take(q)
            if k == 1:
                @pl.when(interior)
                def _():
                    take_back()
                    for j in range(2):
                        wait_back(f, j, *inbound)
                    for q in range(-DEEP, 0):
                        take(q)
                    for q in range(-REACH, 0):
                        first(q)

            if k >= 1:
                for q in rows_of(k - 1):
                    first(q)
            if k >= 3:
                for q in rows_of(k - 3):
                    second(q)
                depth_start(f, k - 3, *outbound)
        for j in range(2):
            wait_cross(f, j, *inbound)
        for q in range(own, own + DEEP):
            take(q)
        for q in range(own - REACH, own + REACH):
            first(q)
        for k in range(own_chunks - 3, own_chunks):
            for q in rows_of(k):
                second(q)
            depth_start(f, k, *outbound)

    def halo_row(q):
        return mirrored(q - own, own + REACH - 1 - q)

    def put(f, q):
        e = e_of(q)
        previous = jnp.where(d > 0, din[f, e].astype(f32), 0.0)
        ext[e] = (load_of(0, f, q) - coup_of(0, q) * previous).astype(bf16)

    def first_layer(f, q):
        w = apply_row(0, q, ext, DEEP).astype(bf16)
        return w, (load_of(1, f, q) - coup_of(1, q) * w.astype(f32)).astype(bf16)

    def second_row(f, q):
        wb[f, r_of(q)] = apply_row(1, q, near, REACH).astype(bf16)

    def down_shallow_first(f):
        @pl.when(d > 0)
        def _():
            wait_inbound(f, down_in)

        @pl.when(interior)
        def _():
            @pl.when(d > 0)
            def _():
                for j in range(2):
                    wait_back(f, j, *down_in)
            for q in range(-DEEP, 0):
                put(f, q)

        for q in range(own + DEEP):
            put(f, q)
        for q in reversed(range(own)):
            w, g = first_layer(f, q)
            wa[f, r_of(q)] = w
            mixed[f, r_of(q)] = g
            if q == own - REACH:
                side_copy(f, *mid).start()

        @pl.when(interior)
        def _():
            side_back(f, *mid).start()

    def down_shallow_second(f):
        for r in range(own):
            near[REACH + r] = mixed[f, r]

        @pl.when(interior)
        def _():
            side_wait(f, 0, *mid)
            for i in range(REACH):
                near[i] = dmid[f, 0, i]

        for k in range(own_chunks):
            if k == own_chunks - 1:
                side_wait(f, 1 - flip, *mid)
                for q in range(own, own + REACH):
                    near[e_of(q) - REACH] = dmid[f, 1 - flip, halo_row(q)]
            for q in rows_of(k):
                second_row(f, q)
            depth_start(f, k, *down_out)
        side_start(f, *wside)

    def mix_row(f, q):
        w, g = first_layer(f, q)
        if 0 <= q < own:
            wa[f, r_of(q)] = w
        near[e_of(q) - REACH] = g

    def down_deep(f):
        wave(
            f, down_in, down_out, functools.partial(put, f), lambda: None,
            functools.partial(mix_row, f), functools.partial(second_row, f),
        )
        side_start(f, *wside)

    def down_deepest(f):
        wait_inbound(f, down_in)
        for q in range(own + DEEP):
            put(f, q)

        @pl.when(interior)
        def _():
            for j in range(2):
                wait_back(f, j, *down_in)
            for q in range(-DEEP, 0):
                put(f, q)
            for q in range(-REACH, 0):
                mix_row(f, q)

        for q in range(own + REACH):
            mix_row(f, q)
        for k in reversed(range(own_chunks)):
            for q in rows_of(k):
                second_row(f, q)
            if k == own_chunks - 1:
                side_copy(f, *wside).start()

        @pl.when(interior)
        def _():
            side_back(f, *wside).start()

    def emit(layer, f, q, value):
        s = value.astype(bf16)
        t, i = place(q)
        front = front_of(f)
        obuf[t - 1, layer, 0, front, lanes(i)] = s[:shots]
        obuf[t - 1, layer, 1, front, lanes(i)] = s[shots:]
        return (coup_of(layer, q) * s.astype(f32)).astype(bf16)

    def coupled(q, value):
        return (coup_of(1, q) * value.astype(bf16).astype(f32)).astype(bf16)

    def finish_row(f, q):
        r = r_of(q)
        hout[f, r] = emit(0, f, q, wa[f, r].astype(f32) - apply_row(0, q, near, REACH))

    def finish(f):
        out_copy(f).start()
        out_local(f).start()

    def up_last(f):
        for q in range(own):
            near[e_of(q) - REACH] = emit(1, f, q, wb[f, r_of(q)].astype(f32))

        @pl.when(interior)
        def _():
            side_wait(f, 0, *wside)
            for i in range(REACH):
                near[i] = coupled(i - REACH, whalo[f, 0, i].astype(f32))

        for k in range(own_chunks):
            if k == own_chunks - 1:
                side_wait(f, 1 - flip, *wside)
                for q in range(own, own + REACH):
                    near[e_of(q) - REACH] = coupled(q, whalo[f, 1 - flip, halo_row(q)].astype(f32))
            for q in rows_of(k):
                finish_row(f, q)
            depth_start(f, k, *up_out)
        finish(f)

    def solve_row(f, q):
        part = apply_row(1, q, ext, DEEP)
        if 0 <= q < own:
            near[e_of(q) - REACH] = emit(1, f, q, wb[f, r_of(q)].astype(f32) - part)
        elif q < 0:
            near[e_of(q) - REACH] = coupled(q, whalo[f, 0, q + REACH].astype(f32) - part)
        else:
            near[e_of(q) - REACH] = coupled(q, whalo[f, 1 - flip, halo_row(q)].astype(f32) - part)

    def up(f):
        def take(q):
            ext[e_of(q)] = uin[f, e_of(q)]

        side_wait(f, 1 - flip, *wside)
        wave(
            f, up_in, up_out, take, lambda: side_wait(f, 0, *wside),
            functools.partial(solve_row, f), functools.partial(finish_row, f),
        )
        finish(f)

    def table_local(slot):
        return pltpu.make_async_copy(kvec.at[slot], kcols.at[slot], k_sem)

    def home_wait(which):
        own_copy(which).wait()
        home_copy(which).wait_recv()
        if which == 0:
            table_local(1).start()
            table_local(1).wait()

    def halo_wait(which):
        slot = 3 * (1 - flip)
        halo_arrival(which, 1 - flip).wait_recv()
        if which == 0:
            table_local(slot).start()
            table_local(slot).wait()

        @pl.when(interior)
        def _():
            halo_arrival(which, 0).wait_recv()
            if which == 0:
                table_local(0).start()
                table_local(0).wait()

    @pl.when(worker)
    def _():
        for which in range(3):
            halo_wait(which)
        for which in range(5):
            home_wait(which)

        @pl.when(shallow)
        def _():
            @pl.loop(0, fronts + 1)
            def _(t):
                @pl.when(t < fronts)
                def _():
                    down_shallow_first(t)

                @pl.when(t == 0)
                def _():
                    home_wait(5)

                @pl.when(t > 0)
                def _():
                    down_shallow_second(t - 1)

        @pl.when(jnp.logical_not(shallow))
        def _():
            home_wait(5)
            for which in (3, 4):
                halo_wait(which)

            @pl.when(deepest)
            def _():
                @pl.loop(0, fronts)
                def _(f):
                    down_deepest(f)

                    @pl.when(f > 0)
                    def _():
                        up_last(f - 1)

            @pl.when(jnp.logical_not(deepest))
            def _():
                @pl.loop(0, fronts)
                def _(f):
                    down_deep(f)

        @pl.when(jnp.logical_not(early))
        def _():
            pl.semaphore_signal(go_sem, inc=1, device_id=(d, l - 1), device_id_type=MESH)

        halo_start(5, jnp.logical_not(early))
        halo_wait(5)

        @pl.when(deepest)
        def _():
            up_last(fronts - 1)

        @pl.when(jnp.logical_not(deepest))
        def _():
            @pl.loop(0, fronts)
            def _(f):
                up(f)

        @pl.loop(0, fronts)
        def _(f):
            @pl.when(shallow)
            def _():
                side_sent(f, *mid)

            side_sent(f, *wside)
            depth_sent(f, *down_out)
            depth_sent(f, *up_out)
            out_copy(f).wait_send()
            out_local(f).wait()

    for which in range(6):
        @pl.when(halo_ok & jnp.logical_not(shallow) if which in (3, 4) else halo_ok)
        def _():
            halo_copy(which).wait_send()


def per_device(right_sides, sources, coupling, block_cols, factors):
    layers, parts, shot_count, cells = right_sides.shape
    rows, stored = block_cols.shape[1:]
    blk = factors.shape[-1]
    lat_count = lax.axis_size("lat")
    assert lax.axis_size("depth") > SHALLOW and layers == 2 and rows == DEEP and parts == 2
    assert lat_count % 2 == 0 and lat_count >= 4
    fronts = FRONTS
    pair = parts * (shot_count // fronts)
    own = 2 * rows
    ext_rows = own + 2 * DEEP
    hops = own // REACH + 4
    bf16 = jnp.bfloat16
    table = block_cols.reshape(layers, rows * stored)
    table = jnp.pad(table, ((0, 8 - layers), (0, 128 - rows * stored)))
    hbm = pl.BlockSpec(memory_space=pltpu.HBM)
    vmem = pl.BlockSpec(memory_space=pltpu.VMEM)
    smem = pl.BlockSpec(memory_space=pltpu.SMEM)
    dma = pltpu.SemaphoreType.DMA
    return pl.pallas_call(
        functools.partial(sweep_kernel, lax.axis_size("depth"), lat_count, fronts),
        out_shape=jax.ShapeDtypeStruct(right_sides.shape, bf16),
        in_specs=[smem, vmem, hbm, hbm, hbm],
        out_specs=hbm,
        scratch_shapes=[
            pltpu.VMEM((ext_rows, pair, blk), bf16),
            pltpu.VMEM((own + 2 * REACH, pair, blk), bf16),
            pltpu.VMEM((fronts, ext_rows, pair, blk), bf16),
            pltpu.VMEM((fronts, ext_rows, pair, blk), bf16),
            pltpu.VMEM((fronts, 2, REACH, pair, blk), bf16),
            pltpu.VMEM((fronts, 2, REACH, pair, blk), bf16),
            pltpu.VMEM((fronts, own, pair, blk), bf16),
            pltpu.VMEM((fronts, own, pair, blk), bf16),
            pltpu.VMEM((fronts, own, pair, blk), bf16),
            pltpu.VMEM((fronts, own, pair, blk), bf16),
            pltpu.VMEM((4,) + right_sides.shape, bf16),
            pltpu.VMEM((4,) + coupling.shape, jnp.float32),
            pltpu.VMEM((layers, own + 2 * REACH) + factors.shape[2:], bf16),
            pltpu.VMEM((2,) + right_sides.shape, bf16),
            pltpu.VMEM((shot_count, blk), jnp.int32),
            pltpu.VMEM((4,) + table.shape, jnp.int32),
            pltpu.SMEM((4,) + table.shape, jnp.int32),
            dma((fronts, hops)), dma((fronts, hops)), dma((fronts, hops)), dma((fronts, hops)),
            dma((fronts, 2)), dma((fronts, 2)), dma((fronts, 2)), dma((fronts, 2)),
            dma((2, 6)), dma((4, 6)), dma((fronts,)), dma((fronts,)), dma, pltpu.SemaphoreType.REGULAR,
        ],
        compiler_params=pltpu.CompilerParams(
            collective_id=0, has_side_effects=True, vmem_limit_bytes=63 * 2**20
        ),
    )(sources, table, right_sides, coupling, factors)


def solution(mesh):
    in_specs = (
        P("depth", None, None, "lat"),
        P(),
        P("depth", "lat"),
        P("depth", "lat", None),
        P("depth", "lat", None, None, None, None),
    )
    out_specs = P("depth", None, None, "lat")
    return jax.shard_map(
        per_device, mesh=mesh, in_specs=in_specs, out_specs=out_specs, check_vma=False
    )
```

```python
import functools

import jax
import jax.numpy as jnp
from jax import lax
from jax.experimental import pallas as pl
from jax.experimental.pallas import tpu as pltpu
from jax.sharding import PartitionSpec as P

REACH = 3
DEEP = 2 * REACH
FRONTS = 4
SHALLOW = 2
HOME = (0, 1, 2, 3, 4, 7, 5)

source_gain = 8.0

MESH = pl.DeviceIdType.MESH


def sweep_kernel(
    depth_count, lat_count, fronts,
    srcs_ref, cols_ref, rhs_ref, coup_ref, fac_ref, out_ref,
    ext, near, din, uin, dmid, whalo, wa, wb, mixed, hout, rbuf, cbuf, facs, obuf, spread, kvec, kcols,
    d_send, d_recv, u_send, u_recv, m_send, m_recv, w_send, w_recv, p_send, p_recv, o_send, o_recv, k_sem, go_sem,
):
    d = lax.axis_index("depth")
    l = lax.axis_index("lat")
    tile, stored, _, blk, _ = fac_ref.shape[1:]
    shot_count = rhs_ref.shape[2]
    shots = shot_count // fronts
    own = 2 * tile
    total_rows = own + 2 * DEEP
    chips = lat_count // 2
    chip = l // 2
    odd = lax.rem(l, 2)
    worker = odd == 1
    flip = chip // (chips - 1)
    interior = (chip > 0) & (chip < chips - 1)
    shallow = d < SHALLOW
    early = d >= depth_count // 2
    deepest = d == depth_count - 1
    bf16, f32 = jnp.bfloat16, jnp.float32

    def mirrored(a, b):
        return a + flip * (b - a)

    def e_of(q):
        return mirrored(q + DEEP, own - 1 - q + DEEP)

    def r_of(q):
        return mirrored(q, own - 1 - q)

    def place(q):
        a, b = q + DEEP, own - 1 - q + DEEP
        return mirrored(a // tile, b // tile), mirrored(a % tile, b % tile)

    def lanes(i):
        return pl.ds(pl.multiple_of(i * blk, blk), blk)

    def front_of(f):
        return pl.ds(pl.multiple_of(f * shots, shots), shots)

    def remote(src, dst, ssem, rsem, dd, to_l):
        return pltpu.make_async_remote_copy(
            src_ref=src, dst_ref=dst, send_sem=ssem, recv_sem=rsem,
            device_id=(d + dd, to_l), device_id_type=MESH,
        )

    def parts_of(which, slot, halo):
        if which == 0:
            return cols_ref, kvec.at[slot]
        if which == 1:
            return coup_ref, cbuf.at[slot]
        if which in (2, 6) and halo:
            some = pl.ds(0, shots) if which == 2 else pl.ds(shots, shot_count - shots)
            return rhs_ref.at[0, :, some], rbuf.at[slot, 0, :, some]
        if which == 2:
            return rhs_ref.at[0], rbuf.at[slot, 0]
        if which == 3 and halo:
            place_ = pl.ds(pl.multiple_of(odd * (tile - REACH) * blk, blk), REACH * blk)
            return rhs_ref.at[1, :, :, place_], rbuf.at[slot, 1, :, :, place_]
        if which == 3:
            return rhs_ref.at[1], rbuf.at[slot, 1]
        layer = which - 4
        if halo:
            first = (1 - odd) * (own + REACH)
            return fac_ref.at[layer, pl.ds(odd * (tile - REACH), REACH)], facs.at[layer, pl.ds(first, REACH)]
        return fac_ref.at[layer], facs.at[layer, pl.ds(REACH + (slot - 1) * tile, tile)]

    def home_copy(which):
        if which in (4, 7):
            first = mirrored(tile - REACH, 0) if which == 4 else mirrored(0, REACH)
            src = fac_ref.at[0, pl.ds(first, REACH)]
            dst = facs.at[0, pl.ds(REACH + first, REACH)]
        else:
            src, dst = parts_of(which, 1, False)
        return remote(src, dst, p_send.at[0, which], p_recv.at[1, which], 0, l + 1)

    def halo_copy(which):
        slot = 3 * (1 - odd)
        src, dst = parts_of(which, slot, True)
        return remote(src, dst, p_send.at[1, which], p_recv.at[slot, which], 0, l - 1 + 3 * odd)

    def halo_arrival(which, high):
        slot = 3 * high
        if which == 3:
            place_ = pl.ds(pl.multiple_of((1 - high) * (tile - REACH) * blk, blk), REACH * blk)
            src, dst = rhs_ref.at[1, :, :, place_], rbuf.at[slot, 1, :, :, place_]
        elif which in (4, 5):
            src = fac_ref.at[which - 4, pl.ds(0, REACH)]
            dst = facs.at[which - 4, pl.ds(high * (own + REACH), REACH)]
        else:
            src, dst = parts_of(which, slot, True)
        return remote(src, dst, p_send.at[1, which], p_recv.at[slot, which], 0, l - 1)

    halo_ok = (l > 0) & (l < lat_count - 1)

    def own_copy(which):
        if which == 0:
            return pltpu.make_async_copy(cols_ref, kcols.at[2], p_recv.at[2, 0])
        src, dst = parts_of(which, 2, False)
        return pltpu.make_async_copy(src, dst, p_recv.at[2, which])

    @pl.when(worker)
    def _():
        for which in range(6):
            own_copy(which).start()

    barrier = pltpu.get_barrier_semaphore()
    total = jnp.int32(0)
    for dd, dl in [(0, -1), (0, 1)] + [(a, b) for a in (-1, 0, 1) for b in (-2, 0, 2) if (a, b) != (0, 0)]:
        ok = (d + dd >= 0) & (d + dd < depth_count) & (l + dl >= 0) & (l + dl < lat_count)
        if dl in (-2, 0, 2):
            ok = ok & worker

        @pl.when(ok)
        def _():
            pl.semaphore_signal(barrier, inc=1, device_id=(d + dd, l + dl), device_id_type=MESH)

        total = total + ok.astype(jnp.int32)

    for shot in range(shot_count):
        spread[pl.ds(shot, 1), :] = jnp.full((1, blk), srcs_ref[shot], jnp.int32)

    pl.semaphore_wait(barrier, total)

    def halo_start(which, also):
        @pl.when(halo_ok & also)
        def _():
            halo_copy(which).start()

    def out_copy(f):
        front = front_of(f)
        return remote(
            obuf.at[0, :, :, front], out_ref.at[:, :, front], o_send.at[f], o_recv.at[f], 0, l - 1 + 2 * (1 - odd)
        )

    def out_local(f):
        front = front_of(f)
        return pltpu.make_async_copy(obuf.at[1, :, :, front], out_ref.at[:, :, front], o_recv.at[f])

    @pl.when(jnp.logical_not(worker))
    def _():
        for which in HOME:
            home_copy(which).start()

    always = d >= 0
    for which in (0, 1, 2, 6):
        halo_start(which, always)
    for which in (3, 4):
        halo_start(which, jnp.logical_not(shallow))
    halo_start(5, early)

    @pl.when(jnp.logical_not(worker))
    def _():
        @pl.when(jnp.logical_not(early))
        def _():
            pl.semaphore_wait(go_sem, 1)

        halo_start(5, jnp.logical_not(early))
        for which in HOME:
            home_copy(which).wait_send()

        @pl.loop(0, fronts)
        def _(f):
            out_copy(f).wait_recv()

    first_row = chip * own
    lane = lax.broadcasted_iota(jnp.int32, (shots, blk), 1)
    first_cell = (first_row - DEEP) * blk

    def load_of(layer, f, q):
        t, i = place(q)
        front = front_of(f)
        spike = jnp.where(spread[front, :] == first_cell + e_of(q) * blk + lane, source_gain, 0.0).astype(f32)
        real = rbuf[t, layer, 0, front, lanes(i)].astype(f32) + spike
        imag = rbuf[t, layer, 1, front, lanes(i)].astype(f32)
        return jnp.concatenate([real, imag], axis=0)

    def coup_of(layer, q):
        t, i = place(q)
        return cbuf[t, pl.ds(layer, 1), lanes(i)]

    def apply_row(layer, q, field, shift):
        t, i = place(q)
        top = field.shape[0] - 1
        xs = [
            field[jnp.clip(kcols[t, layer, n, i] - first_row + shift, 0, top)] for n in range(stored)
        ]
        x = jnp.concatenate(xs, axis=1)
        row = e_of(q) - (DEEP - REACH)
        w = jnp.concatenate(
            [jnp.concatenate([facs[layer, row, n, 0], facs[layer, row, n, 1]], axis=1) for n in range(stored)],
            axis=0,
        )
        p = jnp.dot(x, w, preferred_element_type=f32)
        real = p[:shots, :blk] - p[shots:, blk:]
        imag = p[:shots, blk:] + p[shots:, :blk]
        return jnp.concatenate([real, imag], axis=0)

    last_l = l + 2 - 4 * flip

    own_chunks = own // REACH
    cross_first = own_chunks - DEEP // REACH

    def own_chunk(f, k, src, dst, ssem, rsem, dd):
        a, n = k * REACH, REACH
        r0 = mirrored(a, own - a - n)
        return remote(
            src.at[f, pl.ds(r0, n)], dst.at[f, pl.ds(r0 + DEEP, n)], ssem.at[f, k], rsem.at[f, k], dd, l
        )

    def cross_chunk(f, j, src, dst, ssem, rsem, dd):
        a, n = (cross_first + j) * REACH, REACH
        r0 = mirrored(a, own - a - n)
        e0 = mirrored(a - own + DEEP, own - a - n + own + DEEP)
        return remote(
            src.at[f, pl.ds(r0, n)], dst.at[f, pl.ds(e0, n)],
            ssem.at[f, own_chunks + j], rsem.at[f, own_chunks + 2 * flip + j], dd, last_l,
        )

    def back_chunk(f, j, src, dst, ssem, rsem, dd):
        r0 = REACH * (1 - j)
        return remote(
            src.at[f, pl.ds(r0, REACH)], dst.at[f, pl.ds(r0 + own + DEEP, REACH)],
            ssem.at[f, own_chunks + 2 + j], rsem.at[f, own_chunks + 2 + j], dd, l - 2,
        )

    def wait_chunk(f, slot, e0, n, dst, src, ssem, rsem, dd):
        remote(
            src.at[f, pl.ds(0, n)], dst.at[f, pl.ds(e0, n)], ssem.at[f, 0], rsem.at[f, slot], dd, l
        ).wait_recv()

    def wait_own(f, k, dst, src, ssem, rsem, dd):
        a, n = k * REACH, REACH
        wait_chunk(f, k, DEEP + mirrored(a, own - a - n), n, dst, src, ssem, rsem, dd)

    def wait_cross(f, j, dst, src, ssem, rsem, dd):
        q0 = own + DEEP - REACH * (1 + j)
        e0 = mirrored(q0 + DEEP, own - q0 - REACH + DEEP)
        wait_chunk(f, own_chunks + 2 - 2 * flip + j, e0, REACH, dst, src, ssem, rsem, dd)

    def wait_back(f, j, dst, src, ssem, rsem, dd):
        wait_chunk(f, own_chunks + j, REACH * j, REACH, dst, src, ssem, rsem, dd)

    def depth_start(f, k, src, dst, ssem, rsem, dd):
        args = (src, dst, ssem, rsem, dd)

        @pl.when((d + dd >= 0) & (d + dd < depth_count))
        def _():
            if k >= cross_first:
                cross_chunk(f, k - cross_first, *args).start()
            own_chunk(f, k, *args).start()
            if k == 1:
                @pl.when(interior)
                def _():
                    back_chunk(f, 0, *args).start()
                    back_chunk(f, 1, *args).start()

    def depth_sent(f, src, dst, ssem, rsem, dd):
        args = (src, dst, ssem, rsem, dd)

        @pl.when((d + dd >= 0) & (d + dd < depth_count))
        def _():
            for k in range(own_chunks):
                own_chunk(f, k, *args).wait_send()
            for j in range(2):
                cross_chunk(f, j, *args).wait_send()

            @pl.when(interior)
            def _():
                for j in range(2):
                    back_chunk(f, j, *args).wait_send()

    def wait_inbound(f, args):
        for k in range(own_chunks):
            wait_own(f, k, *args)
        for j in range(2):
            wait_cross(f, j, *args)

    def side_copy(f, src, dst, ssem, rsem):
        r0 = mirrored(own - REACH, 0)
        return remote(src.at[f, pl.ds(r0, REACH)], dst.at[f, flip], ssem.at[f, 0], rsem.at[f, flip], 0, last_l)

    def side_back(f, src, dst, ssem, rsem):
        return remote(src.at[f, pl.ds(0, REACH)], dst.at[f, 1], ssem.at[f, 1], rsem.at[f, 1], 0, l - 2)

    def side_start(f, *args):
        side_copy(f, *args).start()

        @pl.when(interior)
        def _():
            side_back(f, *args).start()

    def side_sent(f, *args):
        side_copy(f, *args).wait_send()

        @pl.when(interior)
        def _():
            side_back(f, *args).wait_send()

    def side_wait(f, side, src, dst, ssem, rsem):
        remote(
            src.at[f, pl.ds(0, REACH)], dst.at[f, side], ssem.at[f, 0], rsem.at[f, side], 0, last_l
        ).wait_recv()

    mid = (mixed, dmid, m_send, m_recv)
    wside = (wb, whalo, w_send, w_recv)
    down_in = (din, wb, d_send, d_recv, -1)
    down_out = (wb, din, d_send, d_recv, 1)
    up_in = (uin, hout, u_send, u_recv, 1)
    up_out = (hout, uin, u_send, u_recv, -1)

    def rows_of(k):
        return range(k * REACH, (k + 1) * REACH)

    def wave(f, inbound, outbound, take, take_back, first, second):
        for k in range(own_chunks):
            wait_own(f, k, *inbound)
            for q in rows_of(k):
                take(q)
            if k == 1:
                @pl.when(interior)
                def _():
                    take_back()
                    for j in range(2):
                        wait_back(f, j, *inbound)
                    for q in range(-DEEP, 0):
                        take(q)
                    for q in range(-REACH, 0):
                        first(q)

            if k >= 1:
                for q in rows_of(k - 1):
                    first(q)
            if k >= 3:
                for q in rows_of(k - 3):
                    second(q)
                depth_start(f, k - 3, *outbound)
        for j in range(2):
            wait_cross(f, j, *inbound)
        for q in range(own, own + DEEP):
            take(q)
        for q in range(own - REACH, own + REACH):
            first(q)
        for k in range(own_chunks - 3, own_chunks):
            for q in rows_of(k):
                second(q)
            depth_start(f, k, *outbound)

    def halo_row(q):
        return mirrored(q - own, own + REACH - 1 - q)

    def put(f, q):
        e = e_of(q)
        previous = jnp.where(d > 0, din[f, e].astype(f32), 0.0)
        ext[e] = (load_of(0, f, q) - coup_of(0, q) * previous).astype(bf16)

    def first_layer(f, q):
        w = apply_row(0, q, ext, DEEP).astype(bf16)
        return w, (load_of(1, f, q) - coup_of(1, q) * w.astype(f32)).astype(bf16)

    def second_row(f, q):
        wb[f, r_of(q)] = apply_row(1, q, near, REACH).astype(bf16)

    def down_shallow_first(f):
        @pl.when(d > 0)
        def _():
            wait_inbound(f, down_in)

        @pl.when(interior)
        def _():
            @pl.when(d > 0)
            def _():
                for j in range(2):
                    wait_back(f, j, *down_in)
            for q in range(-DEEP, 0):
                put(f, q)

        for q in range(own + DEEP):
            put(f, q)
        for q in reversed(range(own)):
            w, g = first_layer(f, q)
            wa[f, r_of(q)] = w
            mixed[f, r_of(q)] = g
            if q == own - REACH:
                side_copy(f, *mid).start()

                @pl.when(f == 0)
                def _():
                    home_wait(7)

        @pl.when(interior)
        def _():
            side_back(f, *mid).start()

    def down_shallow_second(f):
        for r in range(own):
            near[REACH + r] = mixed[f, r]

        @pl.when(interior)
        def _():
            side_wait(f, 0, *mid)
            for i in range(REACH):
                near[i] = dmid[f, 0, i]

        for k in range(own_chunks):
            if k == own_chunks - 1:
                side_wait(f, 1 - flip, *mid)
                for q in range(own, own + REACH):
                    near[e_of(q) - REACH] = dmid[f, 1 - flip, halo_row(q)]
            for q in rows_of(k):
                second_row(f, q)
            depth_start(f, k, *down_out)
        side_start(f, *wside)

    def mix_row(f, q):
        w, g = first_layer(f, q)
        if 0 <= q < own:
            wa[f, r_of(q)] = w
        near[e_of(q) - REACH] = g

    def down_deep(f):
        wave(
            f, down_in, down_out, functools.partial(put, f), lambda: None,
            functools.partial(mix_row, f), functools.partial(second_row, f),
        )
        side_start(f, *wside)

    def down_deepest(f):
        wait_inbound(f, down_in)
        for q in range(own + DEEP):
            put(f, q)

        @pl.when(interior)
        def _():
            for j in range(2):
                wait_back(f, j, *down_in)
            for q in range(-DEEP, 0):
                put(f, q)
            for q in range(-REACH, 0):
                mix_row(f, q)

        for q in range(own + REACH):
            mix_row(f, q)
        for k in reversed(range(own_chunks)):
            for q in rows_of(k):
                second_row(f, q)
            if k == own_chunks - 1:
                side_copy(f, *wside).start()

        @pl.when(interior)
        def _():
            side_back(f, *wside).start()

    def emit(layer, f, q, value):
        s = value.astype(bf16)
        t, i = place(q)
        front = front_of(f)
        obuf[t - 1, layer, 0, front, lanes(i)] = s[:shots]
        obuf[t - 1, layer, 1, front, lanes(i)] = s[shots:]
        return (coup_of(layer, q) * s.astype(f32)).astype(bf16)

    def coupled(q, value):
        return (coup_of(1, q) * value.astype(bf16).astype(f32)).astype(bf16)

    def finish_row(f, q):
        r = r_of(q)
        hout[f, r] = emit(0, f, q, wa[f, r].astype(f32) - apply_row(0, q, near, REACH))

    def finish(f):
        out_copy(f).start()
        out_local(f).start()

    def up_last(f):
        for q in range(own):
            near[e_of(q) - REACH] = emit(1, f, q, wb[f, r_of(q)].astype(f32))

        @pl.when(interior)
        def _():
            side_wait(f, 0, *wside)
            for i in range(REACH):
                near[i] = coupled(i - REACH, whalo[f, 0, i].astype(f32))

        for k in range(own_chunks):
            if k == own_chunks - 1:
                side_wait(f, 1 - flip, *wside)
                for q in range(own, own + REACH):
                    near[e_of(q) - REACH] = coupled(q, whalo[f, 1 - flip, halo_row(q)].astype(f32))
            for q in rows_of(k):
                finish_row(f, q)
            depth_start(f, k, *up_out)
        finish(f)

    def solve_row(f, q):
        part = apply_row(1, q, ext, DEEP)
        if 0 <= q < own:
            near[e_of(q) - REACH] = emit(1, f, q, wb[f, r_of(q)].astype(f32) - part)
        elif q < 0:
            near[e_of(q) - REACH] = coupled(q, whalo[f, 0, q + REACH].astype(f32) - part)
        else:
            near[e_of(q) - REACH] = coupled(q, whalo[f, 1 - flip, halo_row(q)].astype(f32) - part)

    def up(f):
        def take(q):
            ext[e_of(q)] = uin[f, e_of(q)]

        side_wait(f, 1 - flip, *wside)
        wave(
            f, up_in, up_out, take, lambda: side_wait(f, 0, *wside),
            functools.partial(solve_row, f), functools.partial(finish_row, f),
        )
        finish(f)

    def table_local(slot):
        return pltpu.make_async_copy(kvec.at[slot], kcols.at[slot], k_sem)

    def home_wait(which):
        if which < 6:
            own_copy(which).wait()
        home_copy(which).wait_recv()
        if which == 0:
            table_local(1).start()
            table_local(1).wait()

    def halo_wait(which):
        slot = 3 * (1 - flip)
        halo_arrival(which, 1 - flip).wait_recv()
        if which == 0:
            table_local(slot).start()
            table_local(slot).wait()

        @pl.when(interior)
        def _():
            halo_arrival(which, 0).wait_recv()
            if which == 0:
                table_local(0).start()
                table_local(0).wait()

    @pl.when(worker)
    def _():
        for which in range(3):
            halo_wait(which)
        for which in range(5):
            home_wait(which)

        @pl.when(shallow)
        def _():
            @pl.loop(0, fronts + 1)
            def _(t):
                @pl.when(t < fronts)
                def _():
                    down_shallow_first(t)

                @pl.when(t == 0)
                def _():
                    home_wait(5)
                    halo_wait(6)

                @pl.when(t > 0)
                def _():
                    down_shallow_second(t - 1)

        @pl.when(jnp.logical_not(shallow))
        def _():
            for which in (7, 5):
                home_wait(which)
            for which in (6, 3, 4):
                halo_wait(which)

            @pl.when(deepest)
            def _():
                @pl.loop(0, fronts)
                def _(f):
                    down_deepest(f)

                    @pl.when(f > 0)
                    def _():
                        up_last(f - 1)

            @pl.when(jnp.logical_not(deepest))
            def _():
                @pl.loop(0, fronts)
                def _(f):
                    down_deep(f)

        @pl.when(jnp.logical_not(early))
        def _():
            pl.semaphore_signal(go_sem, inc=1, device_id=(d, l - 1), device_id_type=MESH)

        halo_start(5, jnp.logical_not(early))
        halo_wait(5)

        @pl.when(deepest)
        def _():
            up_last(fronts - 1)

        @pl.when(jnp.logical_not(deepest))
        def _():
            @pl.loop(0, fronts)
            def _(f):
                up(f)

        @pl.loop(0, fronts)
        def _(f):
            @pl.when(shallow)
            def _():
                side_sent(f, *mid)

            side_sent(f, *wside)
            depth_sent(f, *down_out)
            depth_sent(f, *up_out)
            out_copy(f).wait_send()
            out_local(f).wait()

    for which in range(7):
        @pl.when(halo_ok & jnp.logical_not(shallow) if which in (3, 4) else halo_ok)
        def _():
            halo_copy(which).wait_send()


def per_device(right_sides, sources, coupling, block_cols, factors):
    layers, parts, shot_count, cells = right_sides.shape
    rows, stored = block_cols.shape[1:]
    blk = factors.shape[-1]
    lat_count = lax.axis_size("lat")
    assert lax.axis_size("depth") > SHALLOW and layers == 2 and rows == DEEP and parts == 2
    assert lat_count % 2 == 0 and lat_count >= 4
    fronts = FRONTS
    pair = parts * (shot_count // fronts)
    own = 2 * rows
    ext_rows = own + 2 * DEEP
    hops = own // REACH + 4
    bf16 = jnp.bfloat16
    hbm = pl.BlockSpec(memory_space=pltpu.HBM)
    vmem = pl.BlockSpec(memory_space=pltpu.VMEM)
    smem = pl.BlockSpec(memory_space=pltpu.SMEM)
    dma = pltpu.SemaphoreType.DMA
    columns = jnp.transpose(block_cols, (0, 2, 1))
    return pl.pallas_call(
        functools.partial(sweep_kernel, lax.axis_size("depth"), lat_count, fronts),
        out_shape=jax.ShapeDtypeStruct(right_sides.shape, bf16),
        in_specs=[smem, hbm, hbm, hbm, hbm],
        out_specs=hbm,
        scratch_shapes=[
            pltpu.VMEM((ext_rows, pair, blk), bf16),
            pltpu.VMEM((own + 2 * REACH, pair, blk), bf16),
            pltpu.VMEM((fronts, ext_rows, pair, blk), bf16),
            pltpu.VMEM((fronts, ext_rows, pair, blk), bf16),
            pltpu.VMEM((fronts, 2, REACH, pair, blk), bf16),
            pltpu.VMEM((fronts, 2, REACH, pair, blk), bf16),
            pltpu.VMEM((fronts, own, pair, blk), bf16),
            pltpu.VMEM((fronts, own, pair, blk), bf16),
            pltpu.VMEM((fronts, own, pair, blk), bf16),
            pltpu.VMEM((fronts, own, pair, blk), bf16),
            pltpu.VMEM((4,) + right_sides.shape, bf16),
            pltpu.VMEM((4,) + coupling.shape, jnp.float32),
            pltpu.VMEM((layers, own + 2 * REACH) + factors.shape[2:], bf16),
            pltpu.VMEM((2,) + right_sides.shape, bf16),
            pltpu.VMEM((shot_count, blk), jnp.int32),
            pltpu.VMEM((4,) + columns.shape, jnp.int32),
            pltpu.SMEM((4,) + columns.shape, jnp.int32),
            dma((fronts, hops)), dma((fronts, hops)), dma((fronts, hops)), dma((fronts, hops)),
            dma((fronts, 2)), dma((fronts, 2)), dma((fronts, 2)), dma((fronts, 2)),
            dma((2, 8)), dma((4, 8)), dma((fronts,)), dma((fronts,)), dma, pltpu.SemaphoreType.REGULAR,
        ],
        compiler_params=pltpu.CompilerParams(
            collective_id=0, has_side_effects=True, vmem_limit_bytes=63 * 2**20
        ),
    )(sources, columns, right_sides, coupling, factors)


def solution(mesh):
    in_specs = (
        P("depth", None, None, "lat"),
        P(),
        P("depth", "lat"),
        P("depth", "lat", None),
        P("depth", "lat", None, None, None, None),
    )
    out_specs = P("depth", None, None, "lat")
    return jax.shard_map(
        per_device, mesh=mesh, in_specs=in_specs, out_specs=out_specs, check_vma=False
    )
```

```python
import functools

import jax
import jax.numpy as jnp
from jax import lax
from jax.experimental import pallas as pl
from jax.experimental.pallas import tpu as pltpu
from jax.sharding import PartitionSpec as P

REACH = 3
DEEP = 2 * REACH
FRONTS = 4
SHALLOW = 2
HOME = (0, 1, 2, 3, 4, 7, 5)

source_gain = 8.0

MESH = pl.DeviceIdType.MESH


def sweep_kernel(
    depth_count, lat_count, fronts,
    srcs_ref, cols_ref, rhs_ref, coup_ref, fac_ref, out_ref,
    ext, near, din, uin, dmid, whalo, wa, wb, mixed, hout, rbuf, cbuf, facs, obuf, spread, kvec, kcols,
    d_send, d_recv, u_send, u_recv, m_send, m_recv, w_send, w_recv, p_send, p_recv, o_send, o_recv, k_sem, go_sem,
):
    d = lax.axis_index("depth")
    l = lax.axis_index("lat")
    tile, stored, _, blk, _ = fac_ref.shape[1:]
    shot_count = rhs_ref.shape[2]
    shots = shot_count // fronts
    own = 2 * tile
    total_rows = own + 2 * DEEP
    chips = lat_count // 2
    chip = l // 2
    odd = lax.rem(l, 2)
    worker = odd == 1
    flip = chip // (chips - 1)
    interior = (chip > 0) & (chip < chips - 1)
    shallow = d < SHALLOW
    early = d >= depth_count // 2
    deepest = d == depth_count - 1
    bf16, f32 = jnp.bfloat16, jnp.float32

    def mirrored(a, b):
        return a + flip * (b - a)

    def e_of(q):
        return mirrored(q + DEEP, own - 1 - q + DEEP)

    def r_of(q):
        return mirrored(q, own - 1 - q)

    def place(q):
        a, b = q + DEEP, own - 1 - q + DEEP
        return mirrored(a // tile, b // tile), mirrored(a % tile, b % tile)

    def lanes(i):
        return pl.ds(pl.multiple_of(i * blk, blk), blk)

    def front_of(f):
        return pl.ds(pl.multiple_of(f * shots, shots), shots)

    def remote(src, dst, ssem, rsem, dd, to_l):
        return pltpu.make_async_remote_copy(
            src_ref=src, dst_ref=dst, send_sem=ssem, recv_sem=rsem,
            device_id=(d + dd, to_l), device_id_type=MESH,
        )

    def parts_of(which, slot, halo):
        if which == 0:
            return cols_ref, kvec.at[slot]
        if which == 1:
            return coup_ref, cbuf.at[slot]
        if which in (2, 6) and halo:
            some = pl.ds(0, shots) if which == 2 else pl.ds(shots, shot_count - shots)
            return rhs_ref.at[0, :, some], rbuf.at[slot, 0, :, some]
        if which == 2:
            return rhs_ref.at[0], rbuf.at[slot, 0]
        if which == 3 and halo:
            place_ = pl.ds(pl.multiple_of(odd * (tile - REACH) * blk, blk), REACH * blk)
            return rhs_ref.at[1, :, :, place_], rbuf.at[slot, 1, :, :, place_]
        if which == 3:
            return rhs_ref.at[1], rbuf.at[slot, 1]
        layer = which - 4
        if halo:
            first = (1 - odd) * (own + REACH)
            return fac_ref.at[layer, pl.ds(odd * (tile - REACH), REACH)], facs.at[layer, pl.ds(first, REACH)]
        return fac_ref.at[layer], facs.at[layer, pl.ds(REACH + (slot - 1) * tile, tile)]

    def home_copy(which):
        if which in (4, 7):
            first = mirrored(tile - REACH, 0) if which == 4 else mirrored(0, REACH)
            src = fac_ref.at[0, pl.ds(first, REACH)]
            dst = facs.at[0, pl.ds(REACH + first, REACH)]
        else:
            src, dst = parts_of(which, 1, False)
        return remote(src, dst, p_send.at[0, which], p_recv.at[1, which], 0, l + 1)

    def halo_copy(which):
        slot = 3 * (1 - odd)
        src, dst = parts_of(which, slot, True)
        return remote(src, dst, p_send.at[1, which], p_recv.at[slot, which], 0, l - 1 + 3 * odd)

    def halo_arrival(which, high):
        slot = 3 * high
        if which == 3:
            place_ = pl.ds(pl.multiple_of((1 - high) * (tile - REACH) * blk, blk), REACH * blk)
            src, dst = rhs_ref.at[1, :, :, place_], rbuf.at[slot, 1, :, :, place_]
        elif which in (4, 5):
            src = fac_ref.at[which - 4, pl.ds(0, REACH)]
            dst = facs.at[which - 4, pl.ds(high * (own + REACH), REACH)]
        else:
            src, dst = parts_of(which, slot, True)
        return remote(src, dst, p_send.at[1, which], p_recv.at[slot, which], 0, l - 1)

    halo_ok = (l > 0) & (l < lat_count - 1)

    def own_copy(which):
        if which == 0:
            return pltpu.make_async_copy(cols_ref, kcols.at[2], p_recv.at[2, 0])
        src, dst = parts_of(which, 2, False)
        return pltpu.make_async_copy(src, dst, p_recv.at[2, which])

    @pl.when(worker)
    def _():
        for which in range(6):
            own_copy(which).start()

    barrier = pltpu.get_barrier_semaphore()
    total = jnp.int32(0)
    for dd, dl in [(0, -1), (0, 1)] + [(a, b) for a in (-1, 0, 1) for b in (-2, 0, 2) if (a, b) != (0, 0)]:
        ok = (d + dd >= 0) & (d + dd < depth_count) & (l + dl >= 0) & (l + dl < lat_count)
        if dl in (-2, 0, 2):
            ok = ok & worker

        @pl.when(ok)
        def _():
            pl.semaphore_signal(barrier, inc=1, device_id=(d + dd, l + dl), device_id_type=MESH)

        total = total + ok.astype(jnp.int32)

    for shot in range(shot_count):
        spread[pl.ds(shot, 1), :] = jnp.full((1, blk), srcs_ref[shot], jnp.int32)

    pl.semaphore_wait(barrier, total)

    def halo_start(which, also):
        @pl.when(halo_ok & also)
        def _():
            halo_copy(which).start()

    def out_copy(f):
        front = front_of(f)
        return remote(
            obuf.at[0, :, :, front], out_ref.at[:, :, front], o_send.at[f], o_recv.at[f], 0, l - 1 + 2 * (1 - odd)
        )

    def out_local(f):
        front = front_of(f)
        return pltpu.make_async_copy(obuf.at[1, :, :, front], out_ref.at[:, :, front], o_recv.at[f])

    @pl.when(jnp.logical_not(worker))
    def _():
        for which in HOME:
            home_copy(which).start()

    always = d >= 0
    for which in (0, 1, 2, 6):
        halo_start(which, always)
    for which in (3, 4):
        halo_start(which, jnp.logical_not(shallow))
    halo_start(5, early)

    @pl.when(jnp.logical_not(worker))
    def _():
        @pl.when(jnp.logical_not(early))
        def _():
            pl.semaphore_wait(go_sem, 1)

        halo_start(5, jnp.logical_not(early))
        for which in HOME:
            home_copy(which).wait_send()

        @pl.loop(0, fronts)
        def _(f):
            out_copy(f).wait_recv()

    first_row = chip * own
    lane = lax.broadcasted_iota(jnp.int32, (shots, blk), 1)
    first_cell = (first_row - DEEP) * blk

    def load_of(layer, f, q):
        t, i = place(q)
        front = front_of(f)
        spike = jnp.where(spread[front, :] == first_cell + e_of(q) * blk + lane, source_gain, 0.0).astype(f32)
        real = rbuf[t, layer, 0, front, lanes(i)].astype(f32) + spike
        imag = rbuf[t, layer, 1, front, lanes(i)].astype(f32)
        return jnp.concatenate([real, imag], axis=0)

    def coup_of(layer, q):
        t, i = place(q)
        return cbuf[t, pl.ds(layer, 1), lanes(i)]

    def apply_row(layer, q, field, shift):
        t, i = place(q)
        top = field.shape[0] - 1
        xs = [
            field[jnp.clip(kcols[t, layer, n, i] - first_row + shift, 0, top)] for n in range(stored)
        ]
        x = jnp.concatenate(xs, axis=1)
        row = e_of(q) - (DEEP - REACH)
        w = jnp.concatenate(
            [jnp.concatenate([facs[layer, row, n, 0], facs[layer, row, n, 1]], axis=1) for n in range(stored)],
            axis=0,
        )
        p = jnp.dot(x, w, preferred_element_type=f32)
        real = p[:shots, :blk] - p[shots:, blk:]
        imag = p[:shots, blk:] + p[shots:, :blk]
        return jnp.concatenate([real, imag], axis=0)

    last_l = l + 2 - 4 * flip

    own_chunks = own // REACH
    cross_first = own_chunks - DEEP // REACH

    def own_chunk(f, k, src, dst, ssem, rsem, dd):
        a, n = k * REACH, REACH
        r0 = mirrored(a, own - a - n)
        return remote(
            src.at[f, pl.ds(r0, n)], dst.at[f, pl.ds(r0 + DEEP, n)], ssem.at[f, k], rsem.at[f, k], dd, l
        )

    def cross_chunk(f, j, src, dst, ssem, rsem, dd):
        a, n = (cross_first + j) * REACH, REACH
        r0 = mirrored(a, own - a - n)
        e0 = mirrored(a - own + DEEP, own - a - n + own + DEEP)
        return remote(
            src.at[f, pl.ds(r0, n)], dst.at[f, pl.ds(e0, n)],
            ssem.at[f, own_chunks + j], rsem.at[f, own_chunks + 2 * flip + j], dd, last_l,
        )

    def back_chunk(f, j, src, dst, ssem, rsem, dd):
        r0 = REACH * (1 - j)
        return remote(
            src.at[f, pl.ds(r0, REACH)], dst.at[f, pl.ds(r0 + own + DEEP, REACH)],
            ssem.at[f, own_chunks + 2 + j], rsem.at[f, own_chunks + 2 + j], dd, l - 2,
        )

    def wait_chunk(f, slot, e0, n, dst, src, ssem, rsem, dd):
        remote(
            src.at[f, pl.ds(0, n)], dst.at[f, pl.ds(e0, n)], ssem.at[f, 0], rsem.at[f, slot], dd, l
        ).wait_recv()

    def wait_own(f, k, dst, src, ssem, rsem, dd):
        a, n = k * REACH, REACH
        wait_chunk(f, k, DEEP + mirrored(a, own - a - n), n, dst, src, ssem, rsem, dd)

    def wait_cross(f, j, dst, src, ssem, rsem, dd):
        q0 = own + DEEP - REACH * (1 + j)
        e0 = mirrored(q0 + DEEP, own - q0 - REACH + DEEP)
        wait_chunk(f, own_chunks + 2 - 2 * flip + j, e0, REACH, dst, src, ssem, rsem, dd)

    def wait_back(f, j, dst, src, ssem, rsem, dd):
        wait_chunk(f, own_chunks + j, REACH * j, REACH, dst, src, ssem, rsem, dd)

    def depth_start(f, k, src, dst, ssem, rsem, dd):
        args = (src, dst, ssem, rsem, dd)

        @pl.when((d + dd >= 0) & (d + dd < depth_count))
        def _():
            if k >= cross_first:
                cross_chunk(f, k - cross_first, *args).start()
            own_chunk(f, k, *args).start()
            if k == 1:
                @pl.when(interior)
                def _():
                    back_chunk(f, 0, *args).start()
                    back_chunk(f, 1, *args).start()

    def depth_sent(f, src, dst, ssem, rsem, dd):
        args = (src, dst, ssem, rsem, dd)

        @pl.when((d + dd >= 0) & (d + dd < depth_count))
        def _():
            for k in range(own_chunks):
                own_chunk(f, k, *args).wait_send()
            for j in range(2):
                cross_chunk(f, j, *args).wait_send()

            @pl.when(interior)
            def _():
                for j in range(2):
                    back_chunk(f, j, *args).wait_send()

    def wait_inbound(f, args):
        for k in range(own_chunks):
            wait_own(f, k, *args)
        for j in range(2):
            wait_cross(f, j, *args)

    def side_copy(f, src, dst, ssem, rsem):
        r0 = mirrored(own - REACH, 0)
        return remote(src.at[f, pl.ds(r0, REACH)], dst.at[f, flip], ssem.at[f, 0], rsem.at[f, flip], 0, last_l)

    def side_back(f, src, dst, ssem, rsem):
        return remote(src.at[f, pl.ds(0, REACH)], dst.at[f, 1], ssem.at[f, 1], rsem.at[f, 1], 0, l - 2)

    def side_start(f, *args):
        side_copy(f, *args).start()

        @pl.when(interior)
        def _():
            side_back(f, *args).start()

    def side_sent(f, *args):
        side_copy(f, *args).wait_send()

        @pl.when(interior)
        def _():
            side_back(f, *args).wait_send()

    def side_wait(f, side, src, dst, ssem, rsem):
        remote(
            src.at[f, pl.ds(0, REACH)], dst.at[f, side], ssem.at[f, 0], rsem.at[f, side], 0, last_l
        ).wait_recv()

    mid = (mixed, dmid, m_send, m_recv)
    wside = (wb, whalo, w_send, w_recv)
    down_in = (din, wb, d_send, d_recv, -1)
    down_out = (wb, din, d_send, d_recv, 1)
    up_in = (uin, hout, u_send, u_recv, 1)
    up_out = (hout, uin, u_send, u_recv, -1)

    def rows_of(k):
        return range(k * REACH, (k + 1) * REACH)

    def wave(f, inbound, outbound, take, take_back, first, second):
        for k in range(own_chunks):
            wait_own(f, k, *inbound)
            for q in rows_of(k):
                take(q)
            if k == 1:
                @pl.when(interior)
                def _():
                    take_back()
                    for j in range(2):
                        wait_back(f, j, *inbound)
                    for q in range(-DEEP, 0):
                        take(q)
                    for q in range(-REACH, 0):
                        first(q)

            if k >= 1:
                for q in rows_of(k - 1):
                    first(q)
            if k >= 3:
                for q in rows_of(k - 3):
                    second(q)
                depth_start(f, k - 3, *outbound)
        for j in range(2):
            wait_cross(f, j, *inbound)
        for q in range(own, own + DEEP):
            take(q)
        for q in range(own - REACH, own + REACH):
            first(q)
        for k in range(own_chunks - 3, own_chunks):
            for q in rows_of(k):
                second(q)
            depth_start(f, k, *outbound)

    def halo_row(q):
        return mirrored(q - own, own + REACH - 1 - q)

    def put(f, q):
        e = e_of(q)
        previous = jnp.where(d > 0, din[f, e].astype(f32), 0.0)
        ext[e] = (load_of(0, f, q) - coup_of(0, q) * previous).astype(bf16)

    def first_layer(f, q):
        w = apply_row(0, q, ext, DEEP).astype(bf16)
        return w, (load_of(1, f, q) - coup_of(1, q) * w.astype(f32)).astype(bf16)

    def second_row(f, q):
        wb[f, r_of(q)] = apply_row(1, q, near, REACH).astype(bf16)

    def down_shallow_first(f):
        @pl.when(d > 0)
        def _():
            wait_inbound(f, down_in)

        @pl.when(interior)
        def _():
            @pl.when(d > 0)
            def _():
                for j in range(2):
                    wait_back(f, j, *down_in)
            for q in range(-DEEP, 0):
                put(f, q)

        for q in range(own + DEEP):
            put(f, q)
        for q in reversed(range(own)):
            w, g = first_layer(f, q)
            wa[f, r_of(q)] = w
            mixed[f, r_of(q)] = g
            if q == own - REACH:
                side_copy(f, *mid).start()

                @pl.when(f == 0)
                def _():
                    home_wait(7)

        @pl.when(interior)
        def _():
            side_back(f, *mid).start()

    def down_shallow_second(f):
        for r in range(own):
            near[REACH + r] = mixed[f, r]

        @pl.when(interior)
        def _():
            side_wait(f, 0, *mid)
            for i in range(REACH):
                near[i] = dmid[f, 0, i]

        for k in range(own_chunks):
            if k == own_chunks - 1:
                side_wait(f, 1 - flip, *mid)
                for q in range(own, own + REACH):
                    near[e_of(q) - REACH] = dmid[f, 1 - flip, halo_row(q)]
            for q in rows_of(k):
                second_row(f, q)
            depth_start(f, k, *down_out)
        side_start(f, *wside)

    def mix_row(f, q):
        w, g = first_layer(f, q)
        if 0 <= q < own:
            wa[f, r_of(q)] = w
        near[e_of(q) - REACH] = g

    def down_deep(f):
        wave(
            f, down_in, down_out, functools.partial(put, f), lambda: None,
            functools.partial(mix_row, f), functools.partial(second_row, f),
        )
        side_start(f, *wside)

    def down_deepest(f):
        wait_inbound(f, down_in)
        for q in range(own + DEEP):
            put(f, q)

        @pl.when(interior)
        def _():
            for j in range(2):
                wait_back(f, j, *down_in)
            for q in range(-DEEP, 0):
                put(f, q)
            for q in range(-REACH, 0):
                mix_row(f, q)

        for q in range(own + REACH):
            mix_row(f, q)
        for k in reversed(range(own_chunks)):
            for q in rows_of(k):
                second_row(f, q)
            if k == own_chunks - 1:
                side_copy(f, *wside).start()

        @pl.when(interior)
        def _():
            side_back(f, *wside).start()

    def emit(layer, f, q, value):
        s = value.astype(bf16)
        t, i = place(q)
        front = front_of(f)
        obuf[t - 1, layer, 0, front, lanes(i)] = s[:shots]
        obuf[t - 1, layer, 1, front, lanes(i)] = s[shots:]
        return (coup_of(layer, q) * s.astype(f32)).astype(bf16)

    def coupled(q, value):
        return (coup_of(1, q) * value.astype(bf16).astype(f32)).astype(bf16)

    def finish_row(f, q):
        r = r_of(q)
        hout[f, r] = emit(0, f, q, wa[f, r].astype(f32) - apply_row(0, q, near, REACH))

    def finish(f):
        out_copy(f).start()
        out_local(f).start()

    def up_last(f):
        for q in range(own):
            near[e_of(q) - REACH] = emit(1, f, q, wb[f, r_of(q)].astype(f32))

        @pl.when(interior)
        def _():
            side_wait(f, 0, *wside)
            for i in range(REACH):
                near[i] = coupled(i - REACH, whalo[f, 0, i].astype(f32))

        for k in range(own_chunks):
            if k == own_chunks - 1:
                side_wait(f, 1 - flip, *wside)
                for q in range(own, own + REACH):
                    near[e_of(q) - REACH] = coupled(q, whalo[f, 1 - flip, halo_row(q)].astype(f32))
            for q in rows_of(k):
                finish_row(f, q)
            depth_start(f, k, *up_out)
        finish(f)

    def solve_row(f, q):
        part = apply_row(1, q, ext, DEEP)
        if 0 <= q < own:
            near[e_of(q) - REACH] = emit(1, f, q, wb[f, r_of(q)].astype(f32) - part)
        elif q < 0:
            near[e_of(q) - REACH] = coupled(q, whalo[f, 0, q + REACH].astype(f32) - part)
        else:
            near[e_of(q) - REACH] = coupled(q, whalo[f, 1 - flip, halo_row(q)].astype(f32) - part)

    def up(f):
        def take(q):
            ext[e_of(q)] = uin[f, e_of(q)]

        side_wait(f, 1 - flip, *wside)
        wave(
            f, up_in, up_out, take, lambda: side_wait(f, 0, *wside),
            functools.partial(solve_row, f), functools.partial(finish_row, f),
        )
        finish(f)

    def table_local(slot):
        return pltpu.make_async_copy(kvec.at[slot], kcols.at[slot], k_sem)

    def home_wait(which):
        if which < 6:
            own_copy(which).wait()
        home_copy(which).wait_recv()
        if which == 0:
            table_local(1).start()
            table_local(1).wait()

    def halo_wait(which):
        slot = 3 * (1 - flip)
        halo_arrival(which, 1 - flip).wait_recv()
        if which == 0:
            table_local(slot).start()
            table_local(slot).wait()

        @pl.when(interior)
        def _():
            halo_arrival(which, 0).wait_recv()
            if which == 0:
                table_local(0).start()
                table_local(0).wait()

    @pl.when(worker)
    def _():
        for which in range(4):
            home_wait(which)
        for which in range(3):
            halo_wait(which)
        home_wait(4)

        behind = jnp.where(d > 0, 0, 1)

        @pl.when(shallow)
        def _():
            @pl.loop(0, fronts + 1)
            def _(t):
                @pl.when(t < fronts)
                def _():
                    down_shallow_first(t)

                @pl.when(t == 0)
                def _():
                    halo_wait(6)

                @pl.when(t == behind)
                def _():
                    home_wait(5)

                @pl.when((t >= behind) & (t < fronts + behind))
                def _():
                    down_shallow_second(t - behind)

        @pl.when(jnp.logical_not(shallow))
        def _():
            for which in (7, 5):
                home_wait(which)
            for which in (6, 3, 4):
                halo_wait(which)

            @pl.when(deepest)
            def _():
                @pl.loop(0, fronts)
                def _(f):
                    down_deepest(f)

                    @pl.when(f > 0)
                    def _():
                        up_last(f - 1)

            @pl.when(jnp.logical_not(deepest))
            def _():
                @pl.loop(0, fronts)
                def _(f):
                    down_deep(f)

        @pl.when(jnp.logical_not(early))
        def _():
            pl.semaphore_signal(go_sem, inc=1, device_id=(d, l - 1), device_id_type=MESH)

        halo_start(5, jnp.logical_not(early))
        halo_wait(5)

        @pl.when(deepest)
        def _():
            up_last(fronts - 1)

        @pl.when(jnp.logical_not(deepest))
        def _():
            @pl.loop(0, fronts)
            def _(f):
                up(f)

        @pl.loop(0, fronts)
        def _(f):
            @pl.when(shallow)
            def _():
                side_sent(f, *mid)

            side_sent(f, *wside)
            depth_sent(f, *down_out)
            depth_sent(f, *up_out)
            out_copy(f).wait_send()
            out_local(f).wait()

    for which in range(7):
        @pl.when(halo_ok & jnp.logical_not(shallow) if which in (3, 4) else halo_ok)
        def _():
            halo_copy(which).wait_send()


def per_device(right_sides, sources, coupling, block_cols, factors):
    layers, parts, shot_count, cells = right_sides.shape
    rows, stored = block_cols.shape[1:]
    blk = factors.shape[-1]
    lat_count = lax.axis_size("lat")
    assert lax.axis_size("depth") > SHALLOW and layers == 2 and rows == DEEP and parts == 2
    assert lat_count % 2 == 0 and lat_count >= 4
    fronts = FRONTS
    pair = parts * (shot_count // fronts)
    own = 2 * rows
    ext_rows = own + 2 * DEEP
    hops = own // REACH + 4
    bf16 = jnp.bfloat16
    hbm = pl.BlockSpec(memory_space=pltpu.HBM)
    vmem = pl.BlockSpec(memory_space=pltpu.VMEM)
    smem = pl.BlockSpec(memory_space=pltpu.SMEM)
    dma = pltpu.SemaphoreType.DMA
    columns = jnp.transpose(block_cols, (0, 2, 1))
    return pl.pallas_call(
        functools.partial(sweep_kernel, lax.axis_size("depth"), lat_count, fronts),
        out_shape=jax.ShapeDtypeStruct(right_sides.shape, bf16),
        in_specs=[smem, hbm, hbm, hbm, hbm],
        out_specs=hbm,
        scratch_shapes=[
            pltpu.VMEM((ext_rows, pair, blk), bf16),
            pltpu.VMEM((own + 2 * REACH, pair, blk), bf16),
            pltpu.VMEM((fronts, ext_rows, pair, blk), bf16),
            pltpu.VMEM((fronts, ext_rows, pair, blk), bf16),
            pltpu.VMEM((fronts, 2, REACH, pair, blk), bf16),
            pltpu.VMEM((fronts, 2, REACH, pair, blk), bf16),
            pltpu.VMEM((fronts, own, pair, blk), bf16),
            pltpu.VMEM((fronts, own, pair, blk), bf16),
            pltpu.VMEM((fronts, own, pair, blk), bf16),
            pltpu.VMEM((fronts, own, pair, blk), bf16),
            pltpu.VMEM((4,) + right_sides.shape, bf16),
            pltpu.VMEM((4,) + coupling.shape, jnp.float32),
            pltpu.VMEM((layers, own + 2 * REACH) + factors.shape[2:], bf16),
            pltpu.VMEM((2,) + right_sides.shape, bf16),
            pltpu.VMEM((shot_count, blk), jnp.int32),
            pltpu.VMEM((4,) + columns.shape, jnp.int32),
            pltpu.SMEM((4,) + columns.shape, jnp.int32),
            dma((fronts, hops)), dma((fronts, hops)), dma((fronts, hops)), dma((fronts, hops)),
            dma((fronts, 2)), dma((fronts, 2)), dma((fronts, 2)), dma((fronts, 2)),
            dma((2, 8)), dma((4, 8)), dma((fronts,)), dma((fronts,)), dma, pltpu.SemaphoreType.REGULAR,
        ],
        compiler_params=pltpu.CompilerParams(
            collective_id=0, has_side_effects=True, vmem_limit_bytes=63 * 2**20
        ),
    )(sources, columns, right_sides, coupling, factors)


def solution(mesh):
    in_specs = (
        P("depth", None, None, "lat"),
        P(),
        P("depth", "lat"),
        P("depth", "lat", None),
        P("depth", "lat", None, None, None, None),
    )
    out_specs = P("depth", None, None, "lat")
    return jax.shard_map(
        per_device, mesh=mesh, in_specs=in_specs, out_specs=out_specs, check_vma=False
    )
```

```python
import functools

import jax
import jax.numpy as jnp
from jax import lax
from jax.experimental import pallas as pl
from jax.experimental.pallas import tpu as pltpu
from jax.sharding import PartitionSpec as P

REACH = 3
DEEP = 2 * REACH
FRONTS = 4
SHALLOW = 2
HOME = (0, 1, 2, 3, 4, 7, 5)

source_gain = 8.0

MESH = pl.DeviceIdType.MESH


def sweep_kernel(
    depth_count, lat_count, fronts,
    srcs_ref, cols_ref, rhs_ref, coup_ref, fac_ref, out_ref,
    ext, near, din, uin, dmid, whalo, wa, wb, mixed, hout, rbuf, cbuf, facs, obuf, spread, kvec, kcols,
    d_send, d_recv, u_send, u_recv, m_send, m_recv, w_send, w_recv, p_send, p_recv, o_send, o_recv, k_sem, go_sem,
):
    d = lax.axis_index("depth")
    l = lax.axis_index("lat")
    tile, stored, _, blk, _ = fac_ref.shape[1:]
    shot_count = rhs_ref.shape[2]
    shots = shot_count // fronts
    own = 2 * tile
    total_rows = own + 2 * DEEP
    chips = lat_count // 2
    chip = l // 2
    odd = lax.rem(l, 2)
    worker = odd == 1
    flip = chip // (chips - 1)
    interior = (chip > 0) & (chip < chips - 1)
    shallow = d < SHALLOW
    early = d >= depth_count // 2
    deepest = d == depth_count - 1
    bf16, f32 = jnp.bfloat16, jnp.float32

    def mirrored(a, b):
        return a + flip * (b - a)

    def e_of(q):
        return mirrored(q + DEEP, own - 1 - q + DEEP)

    def r_of(q):
        return mirrored(q, own - 1 - q)

    def place(q):
        a, b = q + DEEP, own - 1 - q + DEEP
        return mirrored(a // tile, b // tile), mirrored(a % tile, b % tile)

    def lanes(i):
        return pl.ds(pl.multiple_of(i * blk, blk), blk)

    def front_of(f):
        return pl.ds(pl.multiple_of(f * shots, shots), shots)

    def remote(src, dst, ssem, rsem, dd, to_l):
        return pltpu.make_async_remote_copy(
            src_ref=src, dst_ref=dst, send_sem=ssem, recv_sem=rsem,
            device_id=(d + dd, to_l), device_id_type=MESH,
        )

    def parts_of(which, slot, halo):
        if which == 0:
            return cols_ref, kvec.at[slot]
        if which == 1:
            return coup_ref, cbuf.at[slot]
        if which in (2, 6) and halo:
            some = pl.ds(0, shots) if which == 2 else pl.ds(shots, shot_count - shots)
            return rhs_ref.at[0, :, some], rbuf.at[slot, 0, :, some]
        if which == 2:
            return rhs_ref.at[0], rbuf.at[slot, 0]
        if which == 3 and halo:
            place_ = pl.ds(pl.multiple_of(odd * (tile - REACH) * blk, blk), REACH * blk)
            return rhs_ref.at[1, :, :, place_], rbuf.at[slot, 1, :, :, place_]
        if which == 3:
            return rhs_ref.at[1], rbuf.at[slot, 1]
        layer = which - 4
        if halo:
            first = (1 - odd) * (own + REACH)
            return fac_ref.at[layer, pl.ds(odd * (tile - REACH), REACH)], facs.at[layer, pl.ds(first, REACH)]
        return fac_ref.at[layer], facs.at[layer, pl.ds(REACH + (slot - 1) * tile, tile)]

    def home_copy(which):
        if which in (4, 7):
            first = mirrored(tile - REACH, 0) if which == 4 else mirrored(0, REACH)
            src = fac_ref.at[0, pl.ds(first, REACH)]
            dst = facs.at[0, pl.ds(REACH + first, REACH)]
        else:
            src, dst = parts_of(which, 1, False)
        return remote(src, dst, p_send.at[0, which], p_recv.at[1, which], 0, l + 1)

    def halo_copy(which):
        slot = 3 * (1 - odd)
        src, dst = parts_of(which, slot, True)
        return remote(src, dst, p_send.at[1, which], p_recv.at[slot, which], 0, l - 1 + 3 * odd)

    def halo_arrival(which, high):
        slot = 3 * high
        if which == 3:
            place_ = pl.ds(pl.multiple_of((1 - high) * (tile - REACH) * blk, blk), REACH * blk)
            src, dst = rhs_ref.at[1, :, :, place_], rbuf.at[slot, 1, :, :, place_]
        elif which in (4, 5):
            src = fac_ref.at[which - 4, pl.ds(0, REACH)]
            dst = facs.at[which - 4, pl.ds(high * (own + REACH), REACH)]
        else:
            src, dst = parts_of(which, slot, True)
        return remote(src, dst, p_send.at[1, which], p_recv.at[slot, which], 0, l - 1)

    halo_ok = (l > 0) & (l < lat_count - 1)

    def own_copy(which):
        if which == 0:
            return pltpu.make_async_copy(cols_ref, kcols.at[2], p_recv.at[2, 0])
        src, dst = parts_of(which, 2, False)
        return pltpu.make_async_copy(src, dst, p_recv.at[2, which])

    @pl.when(worker)
    def _():
        for which in range(6):
            own_copy(which).start()

    barrier = pltpu.get_barrier_semaphore()
    total = jnp.int32(0)
    for dd, dl in [(0, -1), (0, 1)] + [(a, b) for a in (-1, 0, 1) for b in (-2, 0, 2) if (a, b) != (0, 0)]:
        ok = (d + dd >= 0) & (d + dd < depth_count) & (l + dl >= 0) & (l + dl < lat_count)
        if dl in (-2, 0, 2):
            ok = ok & worker

        @pl.when(ok)
        def _():
            pl.semaphore_signal(barrier, inc=1, device_id=(d + dd, l + dl), device_id_type=MESH)

        total = total + ok.astype(jnp.int32)

    for shot in range(shot_count):
        spread[pl.ds(shot, 1), :] = jnp.full((1, blk), srcs_ref[shot], jnp.int32)

    pl.semaphore_wait(barrier, total)

    def halo_start(which, also):
        @pl.when(halo_ok & also)
        def _():
            halo_copy(which).start()

    def out_copy(f):
        front = front_of(f)
        return remote(
            obuf.at[0, :, :, front], out_ref.at[:, :, front], o_send.at[f], o_recv.at[f], 0, l - 1 + 2 * (1 - odd)
        )

    def out_local(f):
        front = front_of(f)
        return pltpu.make_async_copy(obuf.at[1, :, :, front], out_ref.at[:, :, front], o_recv.at[f])

    @pl.when(jnp.logical_not(worker))
    def _():
        for which in HOME:
            home_copy(which).start()

    always = d >= 0
    for which in (0, 1, 2, 6):
        halo_start(which, always)
    for which in (3, 4):
        halo_start(which, jnp.logical_not(shallow))
    halo_start(5, early)

    @pl.when(jnp.logical_not(worker))
    def _():
        @pl.when(jnp.logical_not(early))
        def _():
            pl.semaphore_wait(go_sem, 1)

        halo_start(5, jnp.logical_not(early))
        for which in HOME:
            home_copy(which).wait_send()

        @pl.loop(0, fronts)
        def _(f):
            out_copy(f).wait_recv()

    first_row = chip * own
    lane = lax.broadcasted_iota(jnp.int32, (shots, blk), 1)
    first_cell = (first_row - DEEP) * blk

    def load_of(layer, f, q):
        t, i = place(q)
        front = front_of(f)
        spike = jnp.where(spread[front, :] == first_cell + e_of(q) * blk + lane, source_gain, 0.0).astype(f32)
        real = rbuf[t, layer, 0, front, lanes(i)].astype(f32) + spike
        imag = rbuf[t, layer, 1, front, lanes(i)].astype(f32)
        return jnp.concatenate([real, imag], axis=0)

    def coup_of(layer, q):
        t, i = place(q)
        return cbuf[t, pl.ds(layer, 1), lanes(i)]

    def apply_row(layer, q, field, shift):
        t, i = place(q)
        top = field.shape[0] - 1
        xs = [
            field[jnp.clip(kcols[t, layer, n, i] - first_row + shift, 0, top)] for n in range(stored)
        ]
        x = jnp.concatenate(xs, axis=1)
        row = e_of(q) - (DEEP - REACH)
        w = jnp.concatenate(
            [jnp.concatenate([facs[layer, row, n, 0], facs[layer, row, n, 1]], axis=1) for n in range(stored)],
            axis=0,
        )
        p = jnp.dot(x, w, preferred_element_type=f32)
        real = p[:shots, :blk] - p[shots:, blk:]
        imag = p[:shots, blk:] + p[shots:, :blk]
        return jnp.concatenate([real, imag], axis=0)

    last_l = l + 2 - 4 * flip

    own_chunks = own // REACH
    cross_first = own_chunks - DEEP // REACH

    def own_chunk(f, k, src, dst, ssem, rsem, dd):
        a, n = k * REACH, REACH
        r0 = mirrored(a, own - a - n)
        return remote(
            src.at[f, pl.ds(r0, n)], dst.at[f, pl.ds(r0 + DEEP, n)], ssem.at[f, k], rsem.at[f, k], dd, l
        )

    def cross_chunk(f, j, src, dst, ssem, rsem, dd):
        a, n = (cross_first + j) * REACH, REACH
        r0 = mirrored(a, own - a - n)
        e0 = mirrored(a - own + DEEP, own - a - n + own + DEEP)
        return remote(
            src.at[f, pl.ds(r0, n)], dst.at[f, pl.ds(e0, n)],
            ssem.at[f, own_chunks + j], rsem.at[f, own_chunks + 2 * flip + j], dd, last_l,
        )

    def back_chunk(f, j, src, dst, ssem, rsem, dd):
        r0 = REACH * (1 - j)
        return remote(
            src.at[f, pl.ds(r0, REACH)], dst.at[f, pl.ds(r0 + own + DEEP, REACH)],
            ssem.at[f, own_chunks + 2 + j], rsem.at[f, own_chunks + 2 + j], dd, l - 2,
        )

    def wait_chunk(f, slot, e0, n, dst, src, ssem, rsem, dd):
        remote(
            src.at[f, pl.ds(0, n)], dst.at[f, pl.ds(e0, n)], ssem.at[f, 0], rsem.at[f, slot], dd, l
        ).wait_recv()

    def wait_own(f, k, dst, src, ssem, rsem, dd):
        a, n = k * REACH, REACH
        wait_chunk(f, k, DEEP + mirrored(a, own - a - n), n, dst, src, ssem, rsem, dd)

    def wait_cross(f, j, dst, src, ssem, rsem, dd):
        q0 = own + DEEP - REACH * (1 + j)
        e0 = mirrored(q0 + DEEP, own - q0 - REACH + DEEP)
        wait_chunk(f, own_chunks + 2 - 2 * flip + j, e0, REACH, dst, src, ssem, rsem, dd)

    def wait_back(f, j, dst, src, ssem, rsem, dd):
        wait_chunk(f, own_chunks + j, REACH * j, REACH, dst, src, ssem, rsem, dd)

    def depth_start(f, k, src, dst, ssem, rsem, dd):
        args = (src, dst, ssem, rsem, dd)

        @pl.when((d + dd >= 0) & (d + dd < depth_count))
        def _():
            if k >= cross_first:
                cross_chunk(f, k - cross_first, *args).start()
            own_chunk(f, k, *args).start()
            if k == 1:
                @pl.when(interior)
                def _():
                    back_chunk(f, 0, *args).start()
                    back_chunk(f, 1, *args).start()

    def depth_sent(f, src, dst, ssem, rsem, dd):
        args = (src, dst, ssem, rsem, dd)

        @pl.when((d + dd >= 0) & (d + dd < depth_count))
        def _():
            for k in range(own_chunks):
                own_chunk(f, k, *args).wait_send()
            for j in range(2):
                cross_chunk(f, j, *args).wait_send()

            @pl.when(interior)
            def _():
                for j in range(2):
                    back_chunk(f, j, *args).wait_send()

    def wait_inbound(f, args):
        for k in range(own_chunks):
            wait_own(f, k, *args)
        for j in range(2):
            wait_cross(f, j, *args)

    def side_copy(f, src, dst, ssem, rsem):
        r0 = mirrored(own - REACH, 0)
        return remote(src.at[f, pl.ds(r0, REACH)], dst.at[f, flip], ssem.at[f, 0], rsem.at[f, flip], 0, last_l)

    def side_back(f, src, dst, ssem, rsem):
        return remote(src.at[f, pl.ds(0, REACH)], dst.at[f, 1], ssem.at[f, 1], rsem.at[f, 1], 0, l - 2)

    def side_start(f, *args):
        side_copy(f, *args).start()

        @pl.when(interior)
        def _():
            side_back(f, *args).start()

    def side_sent(f, *args):
        side_copy(f, *args).wait_send()

        @pl.when(interior)
        def _():
            side_back(f, *args).wait_send()

    def side_wait(f, side, src, dst, ssem, rsem):
        remote(
            src.at[f, pl.ds(0, REACH)], dst.at[f, side], ssem.at[f, 0], rsem.at[f, side], 0, last_l
        ).wait_recv()

    mid = (mixed, dmid, m_send, m_recv)
    wside = (wb, whalo, w_send, w_recv)
    down_in = (din, wb, d_send, d_recv, -1)
    down_out = (wb, din, d_send, d_recv, 1)
    up_in = (uin, hout, u_send, u_recv, 1)
    up_out = (hout, uin, u_send, u_recv, -1)

    def rows_of(k):
        return range(k * REACH, (k + 1) * REACH)

    def wave(f, inbound, outbound, take, take_back, first, second):
        for k in range(own_chunks):
            wait_own(f, k, *inbound)
            for q in rows_of(k):
                take(q)
            if k == 1:
                @pl.when(interior)
                def _():
                    take_back()
                    for j in range(2):
                        wait_back(f, j, *inbound)
                    for q in range(-DEEP, 0):
                        take(q)
                    for q in range(-REACH, 0):
                        first(q)

            if k >= 1:
                for q in rows_of(k - 1):
                    first(q)
            if k >= 3:
                for q in rows_of(k - 3):
                    second(q)
                depth_start(f, k - 3, *outbound)
        for j in range(2):
            wait_cross(f, j, *inbound)
        for q in range(own, own + DEEP):
            take(q)
        for q in range(own - REACH, own + REACH):
            first(q)
        for k in range(own_chunks - 3, own_chunks):
            for q in rows_of(k):
                second(q)
            depth_start(f, k, *outbound)

    def halo_row(q):
        return mirrored(q - own, own + REACH - 1 - q)

    def put(f, q):
        e = e_of(q)
        previous = jnp.where(d > 0, din[f, e].astype(f32), 0.0)
        ext[e] = (load_of(0, f, q) - coup_of(0, q) * previous).astype(bf16)

    def first_layer(f, q):
        w = apply_row(0, q, ext, DEEP).astype(bf16)
        return w, (load_of(1, f, q) - coup_of(1, q) * w.astype(f32)).astype(bf16)

    def second_row(f, q):
        wb[f, r_of(q)] = apply_row(1, q, near, REACH).astype(bf16)

    def down_shallow_first(f):
        @pl.when(d > 0)
        def _():
            wait_inbound(f, down_in)

        @pl.when(interior)
        def _():
            @pl.when(d > 0)
            def _():
                for j in range(2):
                    wait_back(f, j, *down_in)
            for q in range(-REACH, 0):
                put(f, q)

        for q in range(own + REACH):
            put(f, q)
        for q in reversed(range(own)):
            w, g = first_layer(f, q)
            wa[f, r_of(q)] = w
            mixed[f, r_of(q)] = g
            if q == own - REACH:
                side_copy(f, *mid).start()

                @pl.when(f == 0)
                def _():
                    home_wait(7)

        @pl.when(interior)
        def _():
            side_back(f, *mid).start()

    def down_shallow_second(f):
        for r in range(own):
            near[REACH + r] = mixed[f, r]

        @pl.when(interior)
        def _():
            side_wait(f, 0, *mid)
            for i in range(REACH):
                near[i] = dmid[f, 0, i]

        for k in range(own_chunks):
            if k == own_chunks - 1:
                side_wait(f, 1 - flip, *mid)
                for q in range(own, own + REACH):
                    near[e_of(q) - REACH] = dmid[f, 1 - flip, halo_row(q)]
            for q in rows_of(k):
                second_row(f, q)
            depth_start(f, k, *down_out)
        side_start(f, *wside)

    def mix_row(f, q):
        w, g = first_layer(f, q)
        if 0 <= q < own:
            wa[f, r_of(q)] = w
        near[e_of(q) - REACH] = g

    def down_deep(f):
        wave(
            f, down_in, down_out, functools.partial(put, f), lambda: None,
            functools.partial(mix_row, f), functools.partial(second_row, f),
        )
        side_start(f, *wside)

    def down_deepest(f):
        wait_inbound(f, down_in)
        for q in range(own + DEEP):
            put(f, q)

        @pl.when(interior)
        def _():
            for j in range(2):
                wait_back(f, j, *down_in)
            for q in range(-DEEP, 0):
                put(f, q)
            for q in range(-REACH, 0):
                mix_row(f, q)

        for q in range(own + REACH):
            mix_row(f, q)
        for k in reversed(range(own_chunks)):
            for q in rows_of(k):
                second_row(f, q)
            if k == own_chunks - 1:
                side_copy(f, *wside).start()

        @pl.when(interior)
        def _():
            side_back(f, *wside).start()

    def emit(layer, f, q, value):
        s = value.astype(bf16)
        t, i = place(q)
        front = front_of(f)
        obuf[t - 1, layer, 0, front, lanes(i)] = s[:shots]
        obuf[t - 1, layer, 1, front, lanes(i)] = s[shots:]
        return (coup_of(layer, q) * s.astype(f32)).astype(bf16)

    def coupled(q, value):
        return (coup_of(1, q) * value.astype(bf16).astype(f32)).astype(bf16)

    def finish_row(f, q):
        r = r_of(q)
        hout[f, r] = emit(0, f, q, wa[f, r].astype(f32) - apply_row(0, q, near, REACH))

    def finish(f):
        out_copy(f).start()
        out_local(f).start()

    def up_last(f):
        for q in range(own):
            near[e_of(q) - REACH] = emit(1, f, q, wb[f, r_of(q)].astype(f32))

        @pl.when(interior)
        def _():
            side_wait(f, 0, *wside)
            for i in range(REACH):
                near[i] = coupled(i - REACH, whalo[f, 0, i].astype(f32))

        for k in range(own_chunks):
            if k == own_chunks - 1:
                side_wait(f, 1 - flip, *wside)
                for q in range(own, own + REACH):
                    near[e_of(q) - REACH] = coupled(q, whalo[f, 1 - flip, halo_row(q)].astype(f32))
            for q in rows_of(k):
                finish_row(f, q)
            depth_start(f, k, *up_out)
        finish(f)

    def solve_row(f, q):
        part = apply_row(1, q, ext, DEEP)
        if 0 <= q < own:
            near[e_of(q) - REACH] = emit(1, f, q, wb[f, r_of(q)].astype(f32) - part)
        elif q < 0:
            near[e_of(q) - REACH] = coupled(q, whalo[f, 0, q + REACH].astype(f32) - part)
        else:
            near[e_of(q) - REACH] = coupled(q, whalo[f, 1 - flip, halo_row(q)].astype(f32) - part)

    def up(f):
        def take(q):
            ext[e_of(q)] = uin[f, e_of(q)]

        side_wait(f, 1 - flip, *wside)
        wave(
            f, up_in, up_out, take, lambda: side_wait(f, 0, *wside),
            functools.partial(solve_row, f), functools.partial(finish_row, f),
        )
        finish(f)

    def table_local(slot):
        return pltpu.make_async_copy(kvec.at[slot], kcols.at[slot], k_sem)

    def home_wait(which):
        if which < 6:
            own_copy(which).wait()
        home_copy(which).wait_recv()
        if which == 0:
            table_local(1).start()
            table_local(1).wait()

    def halo_wait(which):
        slot = 3 * (1 - flip)
        halo_arrival(which, 1 - flip).wait_recv()
        if which == 0:
            table_local(slot).start()
            table_local(slot).wait()

        @pl.when(interior)
        def _():
            halo_arrival(which, 0).wait_recv()
            if which == 0:
                table_local(0).start()
                table_local(0).wait()

    @pl.when(worker)
    def _():
        for which in range(4):
            home_wait(which)
        for which in range(3):
            halo_wait(which)
        home_wait(4)

        behind = jnp.where(d > 0, 0, 1)

        @pl.when(shallow)
        def _():
            @pl.loop(0, fronts + 1)
            def _(t):
                @pl.when(t < fronts)
                def _():
                    down_shallow_first(t)

                @pl.when(t == 0)
                def _():
                    halo_wait(6)

                @pl.when(t == behind)
                def _():
                    home_wait(5)

                @pl.when((t >= behind) & (t < fronts + behind))
                def _():
                    down_shallow_second(t - behind)

        @pl.when(jnp.logical_not(shallow))
        def _():
            for which in (7, 5):
                home_wait(which)
            for which in (6, 3, 4):
                halo_wait(which)

            @pl.when(deepest)
            def _():
                @pl.loop(0, fronts)
                def _(f):
                    down_deepest(f)

                    @pl.when(f > 0)
                    def _():
                        up_last(f - 1)

            @pl.when(jnp.logical_not(deepest))
            def _():
                @pl.loop(0, fronts)
                def _(f):
                    down_deep(f)

        @pl.when(jnp.logical_not(early))
        def _():
            pl.semaphore_signal(go_sem, inc=1, device_id=(d, l - 1), device_id_type=MESH)

        halo_start(5, jnp.logical_not(early))
        halo_wait(5)

        @pl.when(deepest)
        def _():
            up_last(fronts - 1)

        @pl.when(jnp.logical_not(deepest))
        def _():
            @pl.loop(0, fronts)
            def _(f):
                up(f)

        @pl.loop(0, fronts)
        def _(f):
            @pl.when(shallow)
            def _():
                side_sent(f, *mid)

            side_sent(f, *wside)
            depth_sent(f, *down_out)
            depth_sent(f, *up_out)
            out_copy(f).wait_send()
            out_local(f).wait()

    for which in range(7):
        @pl.when(halo_ok & jnp.logical_not(shallow) if which in (3, 4) else halo_ok)
        def _():
            halo_copy(which).wait_send()


def per_device(right_sides, sources, coupling, block_cols, factors):
    layers, parts, shot_count, cells = right_sides.shape
    rows, stored = block_cols.shape[1:]
    blk = factors.shape[-1]
    lat_count = lax.axis_size("lat")
    assert lax.axis_size("depth") > SHALLOW and layers == 2 and rows == DEEP and parts == 2
    assert lat_count % 2 == 0 and lat_count >= 4
    fronts = FRONTS
    pair = parts * (shot_count // fronts)
    own = 2 * rows
    ext_rows = own + 2 * DEEP
    hops = own // REACH + 4
    bf16 = jnp.bfloat16
    hbm = pl.BlockSpec(memory_space=pltpu.HBM)
    vmem = pl.BlockSpec(memory_space=pltpu.VMEM)
    smem = pl.BlockSpec(memory_space=pltpu.SMEM)
    dma = pltpu.SemaphoreType.DMA
    columns = jnp.transpose(block_cols, (0, 2, 1))
    return pl.pallas_call(
        functools.partial(sweep_kernel, lax.axis_size("depth"), lat_count, fronts),
        out_shape=jax.ShapeDtypeStruct(right_sides.shape, bf16),
        in_specs=[smem, hbm, hbm, hbm, hbm],
        out_specs=hbm,
        scratch_shapes=[
            pltpu.VMEM((ext_rows, pair, blk), bf16),
            pltpu.VMEM((own + 2 * REACH, pair, blk), bf16),
            pltpu.VMEM((fronts, ext_rows, pair, blk), bf16),
            pltpu.VMEM((fronts, ext_rows, pair, blk), bf16),
            pltpu.VMEM((fronts, 2, REACH, pair, blk), bf16),
            pltpu.VMEM((fronts, 2, REACH, pair, blk), bf16),
            pltpu.VMEM((fronts, own, pair, blk), bf16),
            pltpu.VMEM((fronts, own, pair, blk), bf16),
            pltpu.VMEM((fronts, own, pair, blk), bf16),
            pltpu.VMEM((fronts, own, pair, blk), bf16),
            pltpu.VMEM((4,) + right_sides.shape, bf16),
            pltpu.VMEM((4,) + coupling.shape, jnp.float32),
            pltpu.VMEM((layers, own + 2 * REACH) + factors.shape[2:], bf16),
            pltpu.VMEM((2,) + right_sides.shape, bf16),
            pltpu.VMEM((shot_count, blk), jnp.int32),
            pltpu.VMEM((4,) + columns.shape, jnp.int32),
            pltpu.SMEM((4,) + columns.shape, jnp.int32),
            dma((fronts, hops)), dma((fronts, hops)), dma((fronts, hops)), dma((fronts, hops)),
            dma((fronts, 2)), dma((fronts, 2)), dma((fronts, 2)), dma((fronts, 2)),
            dma((2, 8)), dma((4, 8)), dma((fronts,)), dma((fronts,)), dma, pltpu.SemaphoreType.REGULAR,
        ],
        compiler_params=pltpu.CompilerParams(
            collective_id=0, has_side_effects=True, vmem_limit_bytes=63 * 2**20
        ),
    )(sources, columns, right_sides, coupling, factors)


def solution(mesh):
    in_specs = (
        P("depth", None, None, "lat"),
        P(),
        P("depth", "lat"),
        P("depth", "lat", None),
        P("depth", "lat", None, None, None, None),
    )
    out_specs = P("depth", None, None, "lat")
    return jax.shard_map(
        per_device, mesh=mesh, in_specs=in_specs, out_specs=out_specs, check_vma=False
    )
```
